128 devices in a mesh: dp: 8 (over y_lo, z), ctx: 16 (over y_hi, x, core).
Axes of the slice: x: 4, y: 4 (y_hi: 2, y_lo: 2; y = y_hi * 2 + y_lo), z: 4, core: 2. Of those that a mesh axis runs over, the one named last changes fastest.
Arguments:
- queries: bfloat16 [65536, 2048], P(('dp', 'ctx')), parts along dimension 0, may hold values from -72 to 72
- key_rows: bfloat16 [65536, 1024], P(('dp', 'ctx')), parts along dimension 0, may hold values from -6 to 6
- value_rows: bfloat16 [65536, 1024], P(('dp', 'ctx')), parts along dimension 0, may hold values from -6 to 6
- parents: int32 [512], P('dp'), parts along dimension 0, may hold values from 0 to 62, as said below
- kept_tiles: int32 [512], P('dp'), parts along dimension 0, may hold values from 0 to 1, as said below
Outputs:
- attended: bfloat16 [65536, 2048], P(('dp', 'ctx')), parts along dimension 0
The draws below stay inside these ranges and needn't reach their ends.
There are 8 independent parts, one for each index of `dp`. The reference program is written for one: setup_inputs(seed, part) draws one part's arguments, and reference() takes and returns one part's arrays. A program takes and returns all parts, laid end to end along the dimension named above; each array names one. Nothing has to cross between parts.
Inputs may be any that keep to these rules, and one draw needn't show every extreme that they name: parents[b] is one to three less than b for b > 0, and parents[0] = 0. `kept_tiles`: 1 keeps a tile of 128 positions, 0 prunes it; the tiles of one index of ctx keep at most 2 tiles, and some such shard keeps exactly that many.
All inputs are finite; a program needn't handle non-finite values.
Results may differ from the reference program's by a relative error of at most 0.0065.
Values may be sent and summed in bfloat16 or wider, within the bound.
A program may use at most 576 MiB of HBM per device.

```python
import jax
import jax.numpy as jnp
from jax import lax

HEADS = 16
KV_HEADS = 8
HEAD_DIM = 128
WINDOW = 4096
BLK = 128
TOK_DEV = 512
TOKENS = 8192
BLOCKS = 64
N_CTX = 16


def shared_draw(key):
    key_part = jax.random.fold_in(key, 101)
    query_part = jax.random.fold_in(key, 102)
    width_keys = KV_HEADS * HEAD_DIM
    width_queries = HEADS * HEAD_DIM
    keys_out = jax.random.truncated_normal(key_part, -6.0, 6.0, (TOKENS, width_keys), jnp.float32)
    queries_out = jax.random.truncated_normal(query_part, -6.0, 6.0, (TOKENS, width_queries), jnp.float32)
    return (queries_out, keys_out)


def draw_queries(key, part):
    return shared_draw(key)[0].astype(jnp.bfloat16)


def draw_key_rows(key, part):
    return shared_draw(key)[1].astype(jnp.bfloat16)


def draw_parents(key, part):
    tile_number = jnp.arange(BLOCKS, dtype=jnp.int32)
    jumps = jax.random.randint(jax.random.fold_in(key, 201), (BLOCKS,), 1, 4)
    jumps = jnp.where(tile_number == BLOCKS - 1, 1, jumps)
    return jnp.maximum(tile_number - jumps, 0).astype(jnp.int32)


def draw_kept_tiles(key, part):
    shards = TOKENS // TOK_DEV
    tiles_dev = TOK_DEV // BLK
    most_kept = tiles_dev // 2
    counts = jax.random.randint(jax.random.fold_in(key, 301), (shards,), 0, most_kept + 1)
    full_shard = jax.random.randint(jax.random.fold_in(key, 303), (), 0, shards)
    counts = jnp.where(jnp.arange(shards, dtype=jnp.int32) == full_shard, most_kept, counts)
    noise = jax.random.randint(jax.random.fold_in(key, 302), (shards, tiles_dev), 0, 1048576)
    scores = noise * tiles_dev + jnp.arange(tiles_dev, dtype=jnp.int32)[None, :]
    order = jnp.argsort(scores, axis=1, stable=True)
    ranks = jnp.argsort(order, axis=1, stable=True).astype(jnp.int32)
    kept = ranks < counts[:, None]
    return kept.reshape(BLOCKS).astype(jnp.int32)


def shard_levels(own_key, shape, cuts, smallest, top_value):
    factor_of = 1.0
    for dim, blocks in cuts:
        heights = jax.random.uniform(jax.random.fold_in(jax.random.fold_in(own_key, 6), dim), (blocks,), jnp.float32, smallest / len(cuts), top_value / len(cuts))
        factor_of = factor_of * jnp.repeat(jnp.exp(heights), shape[dim] // blocks).reshape((-1,) + (1,) * (len(shape) - 1 - dim))
    return factor_of


def scatter_about(stream_key, extent, deviation, most, cuts=(), held_as=jnp.bfloat16):
    array = deviation * jax.random.normal(stream_key, extent, jnp.float32)
    if cuts:
        array = array * shard_levels(stream_key, extent, cuts, -0.22, 0.18)
    return jnp.clip(array, -most, most).astype(held_as)


def setup_inputs(seed: int = 0, part: int = 0) -> dict:
    key_of = jax.random.split(jax.random.key(seed), 6)
    part_keys = jax.random.split(jax.random.fold_in(key_of[5], part), 6)
    queries = draw_queries(jax.random.fold_in(jax.random.fold_in(key_of[5], part), 71), part)
    key_rows = draw_key_rows(jax.random.fold_in(jax.random.fold_in(key_of[5], part), 71), part)
    value_rows = scatter_about(part_keys[2], (TOKENS, KV_HEADS * HEAD_DIM), 1.0, 6.0, ((0, 16),))
    parents = draw_parents(jax.random.fold_in(jax.random.fold_in(key_of[5], part), 71), part)
    kept_tiles = draw_kept_tiles(jax.random.fold_in(jax.random.fold_in(key_of[5], part), 71), part)
    return {"queries": queries, "key_rows": key_rows, "value_rows": value_rows, "parents": parents, "kept_tiles": kept_tiles}


score_scale = 1.0 / 12.0


def ancestry(parents, kept_tiles):
    count_tiles = parents.shape[0]
    block_index = jnp.arange(count_tiles, dtype=jnp.int32)

    def advance(turn, carried):
        current, reached = carried
        onehot = current[:, None] == block_index[None, :]
        current = jnp.sum(jnp.where(onehot, parents[None, :], 0), axis=1).astype(jnp.int32)
        reached = jnp.logical_or(reached, current[:, None] == block_index[None, :])
        return current, reached

    start_reach = block_index[:, None] == block_index[None, :]
    _, reached = lax.fori_loop(0, WINDOW // BLK, advance, (block_index, start_reach))
    kept = kept_tiles > 0
    return reached & kept[:, None] & kept[None, :]


def reference(queries, key_rows, value_rows, parents, kept_tiles):
    groups = HEADS // KV_HEADS
    visible = ancestry(parents, kept_tiles).astype(jnp.float32)
    query_heads = queries.reshape(TOKENS, KV_HEADS, groups, HEAD_DIM)
    band = WINDOW + TOK_DEV
    front = jnp.zeros((WINDOW, KV_HEADS * HEAD_DIM), key_rows.dtype)
    padded_keys = jnp.concatenate([front, key_rows], 0).reshape(TOKENS + WINDOW, KV_HEADS, HEAD_DIM)
    padded_values = jnp.concatenate([front, value_rows], 0).reshape(TOKENS + WINDOW, KV_HEADS, HEAD_DIM)

    def one_block(block_number):
        first_row = (block_number * TOK_DEV).astype(jnp.int32)
        query_part = lax.dynamic_slice_in_dim(query_heads, first_row, TOK_DEV, 0).astype(jnp.float32)
        key_part = lax.dynamic_slice_in_dim(padded_keys, first_row, band, 0).astype(jnp.float32)
        value_part = lax.dynamic_slice_in_dim(padded_values, first_row, band, 0).astype(jnp.float32)
        query_place = first_row + jnp.arange(TOK_DEV, dtype=jnp.int32)
        key_place = first_row - WINDOW + jnp.arange(band, dtype=jnp.int32)
        query_reach = jnp.take(visible, query_place // BLK, axis=0)
        key_block = jnp.clip(key_place, 0, TOKENS - 1) // BLK
        block_allowed = jnp.take(query_reach, key_block, axis=1) > 0.5
        allowed = block_allowed & (key_place[None, :] >= 0) & (key_place[None, :] <= query_place[:, None])
        allowed = allowed & (query_place[:, None] - key_place[None, :] < WINDOW)
        scores = jnp.einsum("qhgd,khd->hgqk", query_part, key_part) * score_scale
        row_max = jnp.max(jnp.where(allowed, scores, -1e30), axis=-1)
        exp_terms = jnp.where(allowed, jnp.exp(scores - row_max[..., None]), 0.0)
        row_total = jnp.sum(exp_terms, axis=-1)
        weights = lax.optimization_barrier(exp_terms.astype(jnp.bfloat16)).astype(jnp.float32)
        weighted = jnp.einsum("hgqk,khd->hgqd", weights, value_part)
        safe_total = jnp.where(row_total > 0, row_total, 1.0)
        result = jnp.where(row_total[..., None] > 0, weighted / safe_total[..., None], 0.0)
        return result.transpose(2, 0, 1, 3).reshape(TOK_DEV, HEADS * HEAD_DIM).astype(jnp.bfloat16)

    outputs = lax.map(one_block, jnp.arange(N_CTX, dtype=jnp.int32))
    return outputs.reshape(TOKENS, HEADS * HEAD_DIM)
```

```python
import functools

import jax
import jax.numpy as jnp
from jax import lax
from jax.experimental import pallas as pl
from jax.experimental.pallas import tpu as pltpu
from jax.sharding import PartitionSpec as P

HEADS = 16
KV_HEADS = 8
HEAD_DIM = 128
WINDOW = 4096
BLK = 128
TILES_DEV = 4
SLOTS = 2
ROW = 8
BLOCKS = 64
GROUP = 2 * HEAD_DIM
CHUNK = 4
NEG = -1e30
SCALE = 1.4426950408889634 / 12.0
MESH = pl.DeviceIdType.MESH


def place():
    c = lax.axis_index("ctx")
    return c, c // ROW, c % ROW


def peer(row, r):
    return {"ctx": row * ROW + r}


def spread_kernel(
    kept_ref, q_hbm, k_hbm, v_hbm, qg, kvg,
    q_v, k_v, v_v, qs, kvs, in_sem, kv_send, kv_recv, q_send, q_recv, up_send, up_recv, own_sem,
):
    c, row, r = place()
    loads = [
        pltpu.make_async_copy(k_hbm, k_v, in_sem.at[0]),
        pltpu.make_async_copy(v_hbm, v_v, in_sem.at[1]),
        pltpu.make_async_copy(q_hbm, q_v, in_sem.at[2]),
    ]
    for load in loads:
        load.start()
    barrier = pltpu.get_barrier_semaphore()
    for step in range(1, ROW):
        pl.semaphore_signal(barrier, 1, device_id=peer(row, (r + step) % ROW), device_id_type=MESH)
    pl.semaphore_signal(barrier, 1, device_id=peer(1 - row, r), device_id_type=MESH)

    f = [kept_ref[c * TILES_DEV + j] > 0 for j in range(TILES_DEV)]

    def pick(ref, slot, cols):
        t = [ref[j * BLK : (j + 1) * BLK, cols] for j in range(TILES_DEV)]
        if slot == 0:
            return jnp.where(f[0], t[0], jnp.where(f[1], t[1], jnp.where(f[2], t[2], t[3])))
        return jnp.where(f[3], t[3], jnp.where(f[2], t[2], jnp.where(f[1], t[1], t[0])))

    loads[0].wait()
    loads[1].wait()
    for slot in range(SLOTS):
        for h in range(ROW):
            cols = slice(h * HEAD_DIM, (h + 1) * HEAD_DIM)
            kvs[h, slot * BLK : (slot + 1) * BLK, :] = pick(k_v, slot, cols)
            kvs[h, (SLOTS + slot) * BLK : (SLOTS + slot + 1) * BLK, :] = pick(v_v, slot, cols)
    pl.semaphore_wait(barrier, ROW)

    def kv_copy(step):
        to = (r + step) % ROW
        return pltpu.make_async_remote_copy(
            kvs.at[to], kvg.at[ROW + r], kv_send.at[step], kv_recv.at[step],
            device_id=peer(row, to), device_id_type=MESH,
        )

    def q_copy(step):
        to = (r + step) % ROW
        return pltpu.make_async_remote_copy(
            qs.at[to], qg.at[r], q_send.at[step], q_recv.at[step],
            device_id=peer(row, to), device_id_type=MESH,
        )

    def up_copy(step):
        s = (r - step + ROW) % ROW
        src = kvs.at[r] if step == 0 else kvg.at[ROW + s]
        return pltpu.make_async_remote_copy(
            src, kvg.at[s], up_send.at[step], up_recv.at[step],
            device_id=peer(1 - row, r), device_id_type=MESH,
        )

    for step in range(1, ROW):
        kv_copy(step).start()

    @pl.when(row == 0)
    def _():
        up_copy(0).start()

    own_kv = pltpu.make_async_copy(kvs.at[r], kvg.at[ROW + r], own_sem.at[0])
    own_kv.start()
    loads[2].wait()
    for slot in range(SLOTS):
        for h in range(ROW):
            cols = slice(h * GROUP, (h + 1) * GROUP)
            qs[h, slot * BLK : (slot + 1) * BLK, :] = pick(q_v, slot, cols)
    own_q = pltpu.make_async_copy(qs.at[r], qg.at[r], own_sem.at[1])
    own_q.start()
    for step in range(1, ROW):
        kv_copy(step).wait_recv()

        @pl.when(row == 0)
        def _():
            up_copy(step).start()

        if step == 3:
            for other in range(1, ROW):
                q_copy(other).start()
    for step in range(1, ROW):
        q_copy(step).wait_recv()

    @pl.when(row == 1)
    def _():
        for step in range(ROW):
            up_copy(step).wait_recv()

    @pl.when(row == 0)
    def _():
        for step in range(ROW):
            up_copy(step).wait_send()

    for step in range(1, ROW):
        kv_copy(step).wait_send()
        q_copy(step).wait_send()
    own_kv.wait()
    own_q.wait()


def spread(kept, q, k, v):
    rows = q.shape[0]
    anywhere = pl.BlockSpec(memory_space=pl.ANY)
    bf16 = jnp.bfloat16
    dma = pltpu.SemaphoreType.DMA
    return pl.pallas_call(
        spread_kernel,
        out_shape=(
            jax.ShapeDtypeStruct((ROW, SLOTS * BLK, GROUP), bf16),
            jax.ShapeDtypeStruct((2 * ROW, 2 * SLOTS * BLK, HEAD_DIM), bf16),
        ),
        in_specs=[pl.BlockSpec(memory_space=pltpu.SMEM), anywhere, anywhere, anywhere],
        out_specs=(anywhere, anywhere),
        scratch_shapes=[
            pltpu.VMEM((rows, HEADS * HEAD_DIM), bf16),
            pltpu.VMEM((rows, KV_HEADS * HEAD_DIM), bf16),
            pltpu.VMEM((rows, KV_HEADS * HEAD_DIM), bf16),
            pltpu.VMEM((ROW, SLOTS * BLK, GROUP), bf16),
            pltpu.VMEM((ROW, 2 * SLOTS * BLK, HEAD_DIM), bf16),
            dma((3,)), dma((ROW,)), dma((ROW,)), dma((ROW,)), dma((ROW,)), dma((ROW,)), dma((ROW,)), dma((2,)),
        ],
        compiler_params=pltpu.CompilerParams(
            collective_id=1, has_side_effects=True, vmem_limit_bytes=60 << 20
        ),
        name="spread",
    )(kept, q, k, v)


def attend_kernel(parents_ref, kept_ref, qg, kvg, og, up_ref, base_ref, list_ref):
    c, row, r = place()
    end = BLOCKS
    first_tile = row * ROW * TILES_DEV

    up_ref[end] = -BLOCKS * 4
    up_ref[0] = end

    def link(t, _):
        p = parents_ref[t]
        up_ref[t] = jnp.where(kept_ref[p] > 0, p, up_ref[p])
        return 0

    lax.fori_loop(1, BLOCKS, link, 0)

    def locate(s, _):
        before = jnp.int32(0)
        lin = jnp.clip(s - ROW * row + ROW, 0, 2 * ROW - 1)
        for j in range(TILES_DEV):
            t = s * TILES_DEV + j
            base_ref[t] = lin * (2 * SLOTS * BLK) + jnp.minimum(before, SLOTS - 1) * BLK
            before = before + jnp.where(kept_ref[t] > 0, 1, 0)
        return 0

    lax.fori_loop(0, BLOCKS // TILES_DEV, locate, 0)
    base_ref[end] = ROW * 2 * SLOTS * BLK

    def collect(j, count):
        t = first_tile + j
        list_ref[count] = t
        return count + jnp.where(kept_ref[t] > 0, 1, 0)

    count = lax.fori_loop(0, ROW * TILES_DEV, collect, jnp.int32(0))
    rc = lax.broadcasted_iota(jnp.int32, (BLK, BLK), 0) - lax.broadcasted_iota(jnp.int32, (BLK, BLK), 1)
    rc = jnp.concatenate([rc, rc], 0)

    def pair(i, _):
        tiles = [list_ref[2 * i], list_ref[jnp.minimum(2 * i + 1, count - 1)]]
        at = []
        for t in tiles:
            slot = (base_ref[t] // BLK) % SLOTS
            at.append(((t - first_tile) // TILES_DEV, pl.multiple_of(slot * BLK, BLK)))
        heads = []
        for s, a in at:
            q = qg[s, pl.ds(a, BLK), :]
            heads.append(jnp.concatenate([q[:, :HEAD_DIM], q[:, HEAD_DIM:]], 0))

        def more(state):
            return (state[0] >= 0) | (state[1] >= 0)

        def step(state):
            nodes = list(state[:2])
            out = []
            for n in range(2):
                m, l, acc = state[2 + 3 * n : 5 + 3 * n]
                node = nodes[n]
                keys, values, gaps = [], [], []
                for _ in range(CHUNK):
                    ok = node >= 0
                    safe = jnp.where(ok, node, end)
                    base = pl.multiple_of(base_ref[safe], BLK)
                    keys.append(kvg[pl.ds(base, BLK), :])
                    values.append(kvg[pl.ds(base + SLOTS * BLK, BLK), :])
                    gaps.append(jnp.where(ok, (tiles[n] - node) * BLK, -WINDOW))
                    nxt = up_ref[safe]
                    node = jnp.where((nxt < end) & (nxt >= tiles[n] - WINDOW // BLK), nxt, -1)
                nodes[n] = node
                s = lax.dot_general(
                    heads[n], jnp.concatenate(keys, 0), (((1,), (1,)), ((), ())),
                    preferred_element_type=jnp.float32,
                ) * SCALE
                parts = []
                for g in range(CHUNK):
                    gap = rc + gaps[g]
                    fine = (gap >= 0) & (gap < WINDOW)
                    parts.append(jnp.where(fine, s[:, g * BLK : (g + 1) * BLK], NEG))
                top = functools.reduce(jnp.maximum, parts)
                new = jnp.maximum(m, jnp.max(top, axis=1, keepdims=True))
                shrink = jnp.exp2(m - new)
                terms = [jnp.exp2(part - new) for part in parts]
                l = l * shrink + sum(terms)
                w = jnp.concatenate([term.astype(jnp.bfloat16) for term in terms], 1)
                acc = acc * shrink + jnp.dot(
                    w, jnp.concatenate(values, 0), preferred_element_type=jnp.float32
                )
                out += [new, l, acc]
            return (*nodes, *out)

        start = []
        for _ in range(2):
            start += [
                jnp.full((2 * BLK, 1), NEG, jnp.float32),
                jnp.zeros((2 * BLK, BLK), jnp.float32),
                jnp.zeros((2 * BLK, HEAD_DIM), jnp.float32),
            ]
        end_state = lax.while_loop(more, step, (tiles[0], tiles[1], *start))
        for n in range(2):
            _, l, acc = end_state[2 + 3 * n : 5 + 3 * n]
            total = jnp.sum(l, axis=1, keepdims=True)
            o = (acc / total).astype(jnp.bfloat16)
            s, a = at[n]
            og[s, pl.ds(a, BLK), :] = jnp.concatenate([o[:BLK], o[BLK:]], 1)
        return 0

    lax.fori_loop(0, (count + 1) // 2, pair, 0)


def attend(parents, kept, qg, kvg):
    smem = pl.BlockSpec(memory_space=pltpu.SMEM)
    vmem = pl.BlockSpec(memory_space=pltpu.VMEM)
    return pl.pallas_call(
        attend_kernel,
        out_shape=jax.ShapeDtypeStruct((ROW, SLOTS * BLK, GROUP), jnp.bfloat16),
        in_specs=[smem, smem, vmem, vmem],
        out_specs=vmem,
        scratch_shapes=[
            pltpu.SMEM((BLOCKS + 1,), jnp.int32),
            pltpu.SMEM((BLOCKS + 1,), jnp.int32),
            pltpu.SMEM((ROW * TILES_DEV + 1,), jnp.int32),
        ],
        compiler_params=pltpu.CompilerParams(vmem_limit_bytes=32 << 20),
        name="attend",
    )(parents, kept, qg, kvg.reshape(2 * ROW * 2 * SLOTS * BLK, HEAD_DIM))


def collect_kernel(og, oc, send, recv, own_sem):
    _, row, r = place()
    barrier = pltpu.get_barrier_semaphore()
    for step in range(1, ROW):
        pl.semaphore_signal(barrier, 1, device_id=peer(row, (r + step) % ROW), device_id_type=MESH)
    own = pltpu.make_async_copy(og.at[r], oc.at[r], own_sem)
    own.start()
    pl.semaphore_wait(barrier, ROW - 1)
    copies = []
    for step in range(1, ROW):
        to = (r + step) % ROW
        copies.append(
            pltpu.make_async_remote_copy(
                og.at[to], oc.at[r], send.at[step], recv.at[step],
                device_id=peer(row, to), device_id_type=MESH,
            )
        )
    for copy in copies:
        copy.start()
    for copy in copies:
        copy.wait_recv()
    for copy in copies:
        copy.wait_send()
    own.wait()


def collect(og):
    anywhere = pl.BlockSpec(memory_space=pl.ANY)
    vmem = pl.BlockSpec(memory_space=pltpu.VMEM)
    return pl.pallas_call(
        collect_kernel,
        out_shape=jax.ShapeDtypeStruct((ROW, SLOTS * BLK, GROUP), jnp.bfloat16),
        in_specs=[vmem],
        out_specs=vmem,
        scratch_shapes=[
            pltpu.SemaphoreType.DMA((ROW,)), pltpu.SemaphoreType.DMA((ROW,)), pltpu.SemaphoreType.DMA,
        ],
        compiler_params=pltpu.CompilerParams(collective_id=2, has_side_effects=True),
        name="collect",
    )(og)


def expand_kernel(kept_ref, oc, out, wide, sem):
    c, _, _ = place()
    copies = []
    before = jnp.bool_(False)
    for j in range(TILES_DEV):
        rows = slice(j * BLK, (j + 1) * BLK)
        kept = kept_ref[c * TILES_DEV + j] > 0
        slot = pl.multiple_of(jnp.where(before, BLK, 0), BLK)

        @pl.when(kept)
        def _():
            for h in range(ROW):
                wide[rows, h * GROUP : (h + 1) * GROUP] = oc[h, pl.ds(slot, BLK), :]

        @pl.when(jnp.logical_not(kept))
        def _():
            wide[rows, :] = jnp.zeros((BLK, HEADS * HEAD_DIM), jnp.bfloat16)

        before = before | kept
        copies.append(pltpu.make_async_copy(wide.at[rows], out.at[rows], sem.at[j]))
        copies[-1].start()
    for copy in copies:
        copy.wait()


def expand(kept, oc):
    rows = TILES_DEV * BLK
    return pl.pallas_call(
        expand_kernel,
        out_shape=jax.ShapeDtypeStruct((rows, HEADS * HEAD_DIM), jnp.bfloat16),
        in_specs=[pl.BlockSpec(memory_space=pltpu.SMEM), pl.BlockSpec(memory_space=pltpu.VMEM)],
        out_specs=pl.BlockSpec(memory_space=pl.ANY),
        scratch_shapes=[
            pltpu.VMEM((rows, HEADS * HEAD_DIM), jnp.bfloat16), pltpu.SemaphoreType.DMA((TILES_DEV,)),
        ],
        name="expand",
    )(kept, oc)


def body(queries, key_rows, value_rows, parents, kept_tiles):
    qg, kvg = spread(kept_tiles, queries, key_rows, value_rows)
    og = attend(parents, kept_tiles, qg, kvg)
    return expand(kept_tiles, collect(og))


def solution(mesh):
    return jax.shard_map(
        body,
        mesh=mesh,
        in_specs=(
            P(("dp", "ctx"), None),
            P(("dp", "ctx"), None),
            P(("dp", "ctx"), None),
            P("dp"),
            P("dp"),
        ),
        out_specs=P(("dp", "ctx"), None),
        check_vma=False,
    )
```

```python
import functools

import jax
import jax.numpy as jnp
from jax import lax
from jax.experimental import pallas as pl
from jax.experimental.pallas import tpu as pltpu
from jax.sharding import PartitionSpec as P

HEADS = 16
KV_HEADS = 8
HEAD_DIM = 128
WINDOW = 4096
BLK = 128
TILES_DEV = 4
SLOTS = 2
ROW = 8
BLOCKS = 64
GROUP = 2 * HEAD_DIM
MOST = 18
SIZES = (2, 4, 6, 8, 10, 12, 18)
PAD = 16
NQ = 2
NEG = -1e30
SCALE = 1.4426950408889634 / 12.0
MESH = pl.DeviceIdType.MESH
STEPS = ((0, 0), (0, 1), (1, 0), (3, 0), (1, 1), (3, 1), (2, 0), (2, 1))
Q_AFTER = 3


def place():
    c = lax.axis_index("ctx")
    return c, c // ROW, c % ROW


def peer(row, r):
    return {"ctx": row * ROW + r}


def ahead(r, step):
    dx, flip = STEPS[step]
    return (r // 2 + dx) % 4 * 2 + (r + flip) % 2


def behind(r, step):
    dx, flip = STEPS[step]
    return (r // 2 + 4 - dx) % 4 * 2 + (r + flip) % 2


def spread_kernel(
    kept_ref, q_hbm, k_hbm, v_hbm, qg, kvg,
    q_v, k_v, v_v, qs, kvs, in_sem, kv_send, kv_recv, q_send, q_recv, up_send, up_recv, own_sem,
):
    c, row, r = place()
    loads = [
        pltpu.make_async_copy(k_hbm, k_v, in_sem.at[0]),
        pltpu.make_async_copy(v_hbm, v_v, in_sem.at[1]),
        pltpu.make_async_copy(q_hbm, q_v, in_sem.at[2]),
    ]
    for load in loads:
        load.start()
    barrier = pltpu.get_barrier_semaphore()
    for step in range(1, ROW):
        pl.semaphore_signal(barrier, 1, device_id=peer(row, (r + step) % ROW), device_id_type=MESH)
    pl.semaphore_signal(barrier, 1, device_id=peer(1 - row, r), device_id_type=MESH)

    f = [kept_ref[c * TILES_DEV + j] > 0 for j in range(TILES_DEV)]

    def pick(ref, slot, cols):
        t = [ref[j * BLK : (j + 1) * BLK, cols] for j in range(TILES_DEV)]
        if slot == 0:
            return jnp.where(f[0], t[0], jnp.where(f[1], t[1], jnp.where(f[2], t[2], t[3])))
        return jnp.where(f[3], t[3], jnp.where(f[2], t[2], jnp.where(f[1], t[1], t[0])))

    def kv_copy(step):
        to = (r + step) % ROW
        return pltpu.make_async_remote_copy(
            kvs.at[to], kvg.at[ROW + r], kv_send.at[step], kv_recv.at[step],
            device_id=peer(row, to), device_id_type=MESH,
        )

    def q_copy(step):
        to = (r + step) % ROW
        return pltpu.make_async_remote_copy(
            qs.at[to], qg.at[r], q_send.at[step], q_recv.at[step],
            device_id=peer(row, to), device_id_type=MESH,
        )

    def up_copy(step):
        s = (r - step + ROW) % ROW
        src = kvs.at[r] if step == 0 else kvg.at[ROW + s]
        return pltpu.make_async_remote_copy(
            src, kvg.at[s], up_send.at[step], up_recv.at[step],
            device_id=peer(1 - row, r), device_id_type=MESH,
        )

    def pack_kv(h):
        cols = pl.ds(pl.multiple_of(h * HEAD_DIM, HEAD_DIM), HEAD_DIM)
        for slot in range(SLOTS):
            kvs[h, slot * BLK : (slot + 1) * BLK, :] = pick(k_v, slot, cols)
            kvs[h, (SLOTS + slot) * BLK : (SLOTS + slot + 1) * BLK, :] = pick(v_v, slot, cols).T

    def pack_q(h):
        for slot in range(SLOTS):
            for g in range(2):
                cols = pl.ds(pl.multiple_of(h * GROUP + g * HEAD_DIM, HEAD_DIM), HEAD_DIM)
                at = slot * 2 * BLK + g * BLK
                qs[h, :, at : at + BLK] = pick(q_v, slot, cols).T

    def kv_copy(step):
        to = ahead(r, step)
        return pltpu.make_async_remote_copy(
            kvs.at[to], kvg.at[ROW + r], kv_send.at[step], kv_recv.at[step],
            device_id=peer(row, to), device_id_type=MESH,
        )

    def q_copy(step):
        to = ahead(r, step)
        return pltpu.make_async_remote_copy(
            qs.at[to], qg.at[r], q_send.at[step], q_recv.at[step],
            device_id=peer(row, to), device_id_type=MESH,
        )

    def up_copy(step):
        s = behind(r, step)
        src = kvs.at[r] if step == 0 else kvg.at[ROW + s]
        return pltpu.make_async_remote_copy(
            src, kvg.at[s], up_send.at[step], up_recv.at[step],
            device_id=peer(1 - row, r), device_id_type=MESH,
        )

    def pass_up(step):
        @pl.when(row == 0)
        def _():
            up_copy(step).start()

    loads[0].wait()
    loads[1].wait()
    pack_kv(r)
    own_kv = pltpu.make_async_copy(kvs.at[r], kvg.at[ROW + r], own_sem.at[0])
    own_kv.start()
    pack_kv(ahead(r, 1))
    pl.semaphore_wait(barrier, ROW)
    pass_up(0)
    for step in range(1, ROW):
        if step > 1:
            pack_kv(ahead(r, step))
        kv_copy(step).start()
    loads[2].wait()
    for step in range(ROW):
        pack_q(ahead(r, step))
    own_q = pltpu.make_async_copy(qs.at[r], qg.at[r], own_sem.at[1])
    own_q.start()
    for step in range(1, ROW):
        kv_copy(step).wait_recv()
        pass_up(step)
        if step == Q_AFTER:
            for other in range(1, ROW):
                q_copy(other).start()
    for step in range(1, ROW):
        q_copy(step).wait_recv()

    @pl.when(row == 1)
    def _():
        for step in range(ROW):
            up_copy(step).wait_recv()

    @pl.when(row == 0)
    def _():
        for step in range(ROW):
            up_copy(step).wait_send()

    for step in range(1, ROW):
        kv_copy(step).wait_send()
        q_copy(step).wait_send()
    own_kv.wait()
    own_q.wait()


def spread(kept, q, k, v):
    rows = q.shape[0]
    anywhere = pl.BlockSpec(memory_space=pl.ANY)
    bf16 = jnp.bfloat16
    dma = pltpu.SemaphoreType.DMA
    return pl.pallas_call(
        spread_kernel,
        out_shape=(
            jax.ShapeDtypeStruct((ROW, HEAD_DIM, SLOTS * 2 * BLK), bf16),
            jax.ShapeDtypeStruct((2 * ROW, 2 * SLOTS * BLK, HEAD_DIM), bf16),
        ),
        in_specs=[pl.BlockSpec(memory_space=pltpu.SMEM), anywhere, anywhere, anywhere],
        out_specs=(anywhere, anywhere),
        scratch_shapes=[
            pltpu.VMEM((rows, HEADS * HEAD_DIM), bf16),
            pltpu.VMEM((rows, KV_HEADS * HEAD_DIM), bf16),
            pltpu.VMEM((rows, KV_HEADS * HEAD_DIM), bf16),
            pltpu.VMEM((ROW, HEAD_DIM, SLOTS * 2 * BLK), bf16),
            pltpu.VMEM((ROW, 2 * SLOTS * BLK, HEAD_DIM), bf16),
            dma((3,)), dma((ROW,)), dma((ROW,)), dma((ROW,)), dma((ROW,)), dma((ROW,)), dma((ROW,)), dma((2,)),
        ],
        compiler_params=pltpu.CompilerParams(
            collective_id=1, has_side_effects=True, vmem_limit_bytes=60 << 20
        ),
        name="spread",
    )(kept, q, k, v)


def attend_kernel(
    parents_ref, kept_ref, qg, kvg, og,
    q_v, kv_v, o_v, bias_ref, up_ref, base_ref, list_ref, seen_ref, size_ref, in_sem, out_sem,
):
    c, row, r = place()
    half = ROW * 2 * SLOTS * BLK
    load_own = pltpu.make_async_copy(kvg.at[half:], kv_v.at[half:], in_sem.at[0])
    load_low = pltpu.make_async_copy(kvg.at[:half], kv_v.at[:half], in_sem.at[1])
    load_q = pltpu.make_async_copy(qg, q_v, in_sem.at[2])
    load_q.start()
    load_own.start()

    @pl.when(row == 1)
    def _():
        load_low.start()

    end = BLOCKS
    reach = WINDOW // BLK
    first_tile = row * ROW * TILES_DEV

    up_ref[end] = -BLOCKS * 4
    up_ref[0] = end
    for t in range(1, BLOCKS):
        p = parents_ref[t]
        up_ref[t] = jnp.where(kept_ref[p] > 0, p, up_ref[p])
    base_ref[end] = half
    for s in range(BLOCKS // TILES_DEV):
        lin = jnp.clip(s - ROW * row + ROW, 0, 2 * ROW - 1) * (2 * SLOTS * BLK)
        before = jnp.int32(0)
        for j in range(TILES_DEV):
            t = s * TILES_DEV + j
            base_ref[t] = lin + jnp.minimum(before, SLOTS - 1) * BLK
            before = before + jnp.where(kept_ref[t] > 0, 1, 0)
    count = jnp.int32(0)
    for j in range(ROW * TILES_DEV):
        t = first_tile + j
        list_ref[count] = t
        count = count + jnp.where(kept_ref[t] > 0, 1, 0)

    def gather(i, _):
        t = list_ref[i]

        def visit(state):
            node, k = state
            seen_ref[i * MOST + k] = base_ref[node] + jnp.where(t - node == reach, 2, 0)
            nxt = up_ref[node]
            return jnp.where(nxt >= t - reach, nxt, end), k + 1

        _, k = lax.while_loop(lambda state: state[0] < end, visit, (t, jnp.int32(0)))
        size_ref[i] = k
        for extra in range(PAD):
            seen_ref[i * MOST + k + extra] = base_ref[end] + 1
        return 0

    lax.fori_loop(0, count, gather, 0)
    rc = lax.broadcasted_iota(jnp.int32, (BLK, BLK), 1) - lax.broadcasted_iota(jnp.int32, (BLK, BLK), 0)
    bias_ref[0] = jnp.zeros((BLK, BLK), jnp.float32)
    bias_ref[1] = jnp.full((BLK, BLK), NEG, jnp.float32)
    bias_ref[2] = jnp.where(rc < 0, 0.0, NEG)
    bias_ref[3] = jnp.where(rc >= 0, 0.0, NEG)
    load_q.wait()
    load_own.wait()

    @pl.when(row == 1)
    def _():
        load_low.wait()

    def some(j, _):
        which = [jnp.minimum(NQ * j + n, count - 1) for n in range(NQ)]
        spots, heads = [], []
        for i in which:
            t = list_ref[i]
            slot = (base_ref[t] // BLK) % SLOTS
            shard = (t - first_tile) // TILES_DEV
            spots.append((shard, pl.multiple_of(slot * BLK, BLK)))
            heads.append(q_v[shard, :, pl.ds(pl.multiple_of(slot * 2 * BLK, 2 * BLK), 2 * BLK)])
        longest = functools.reduce(jnp.maximum, [size_ref[i] for i in which])

        def over(size):
            parts = [[] for _ in which]
            values = [[] for _ in which]
            for n, i in enumerate(which):
                for g in range(size):
                    entry = seen_ref[i * MOST + g]
                    base = pl.multiple_of(entry // BLK * BLK, BLK)
                    bias = bias_ref[3 if g == 0 else entry % BLK]
                    s = jnp.dot(kv_v[pl.ds(base, BLK), :], heads[n], preferred_element_type=jnp.float32) * SCALE
                    parts[n].append(s + jnp.concatenate([bias, bias], 1))
                    values[n].append(kv_v[pl.ds(base + SLOTS * BLK, BLK), :])
            tops = [jnp.max(functools.reduce(jnp.maximum, part), axis=0, keepdims=True) for part in parts]
            accs, totals = [], []
            for n in range(NQ):
                terms = [jnp.exp2(part - tops[n]) for part in parts[n]]
                w = jnp.concatenate([term.astype(jnp.bfloat16) for term in terms], 0)
                totals.append(jnp.sum(functools.reduce(jnp.add, terms), axis=0, keepdims=True))
                accs.append(jnp.dot(jnp.concatenate(values[n], 1), w, preferred_element_type=jnp.float32))
            outs = [(acc / total).astype(jnp.bfloat16) for acc, total in zip(accs, totals)]
            outs = [jnp.concatenate([o[:, :BLK].T, o[:, BLK:].T], 1) for o in outs]
            for i, o in zip(which, outs):
                o_v[i] = o

        for low, size in zip((0, *SIZES), SIZES):
            pl.when((longest > low) & (longest <= size))(functools.partial(over, size))
        for n in range(NQ):

            @pl.when(NQ * j + n < count)
            def _():
                shard, at = spots[n]
                pltpu.make_async_copy(
                    o_v.at[which[n]], og.at[shard, pl.ds(at, BLK), :], out_sem.at[which[n]]
                ).start()

        return 0

    lax.fori_loop(0, (count + NQ - 1) // NQ, some, 0)

    def drain(w, _):
        pltpu.make_async_copy(o_v.at[w], og.at[0, pl.ds(0, BLK), :], out_sem.at[w]).wait()
        return 0

    lax.fori_loop(0, count, drain, 0)


def attend(parents, kept, qg, kvg):
    smem = pl.BlockSpec(memory_space=pltpu.SMEM)
    anywhere = pl.BlockSpec(memory_space=pl.ANY)
    bf16 = jnp.bfloat16
    rows = 2 * ROW * 2 * SLOTS * BLK
    return pl.pallas_call(
        attend_kernel,
        out_shape=jax.ShapeDtypeStruct((ROW, SLOTS * BLK, GROUP), bf16),
        in_specs=[smem, smem, anywhere, anywhere],
        out_specs=anywhere,
        scratch_shapes=[
            pltpu.VMEM((ROW, HEAD_DIM, SLOTS * 2 * BLK), bf16),
            pltpu.VMEM((rows, HEAD_DIM), bf16),
            pltpu.VMEM((ROW * SLOTS, BLK, GROUP), bf16),
            pltpu.VMEM((4, BLK, BLK), jnp.float32),
            pltpu.SMEM((BLOCKS + 1,), jnp.int32),
            pltpu.SMEM((BLOCKS + 1,), jnp.int32),
            pltpu.SMEM((ROW * TILES_DEV + 1,), jnp.int32),
            pltpu.SMEM((ROW * SLOTS * MOST + PAD,), jnp.int32),
            pltpu.SMEM((ROW * SLOTS,), jnp.int32),
            pltpu.SemaphoreType.DMA((3,)),
            pltpu.SemaphoreType.DMA((ROW * SLOTS,)),
        ],
        compiler_params=pltpu.CompilerParams(vmem_limit_bytes=60 << 20),
        name="attend",
    )(parents, kept, qg, kvg.reshape(rows, HEAD_DIM))


def collect_kernel(og, oc, send, recv, own_sem):
    _, row, r = place()
    barrier = pltpu.get_barrier_semaphore()
    for step in range(1, ROW):
        pl.semaphore_signal(barrier, 1, device_id=peer(row, (r + step) % ROW), device_id_type=MESH)
    own = pltpu.make_async_copy(og.at[r], oc.at[r], own_sem)
    own.start()
    pl.semaphore_wait(barrier, ROW - 1)
    copies = []
    for step in range(1, ROW):
        to = (r + step) % ROW
        copies.append(
            pltpu.make_async_remote_copy(
                og.at[to], oc.at[r], send.at[step], recv.at[step],
                device_id=peer(row, to), device_id_type=MESH,
            )
        )
    for copy in copies:
        copy.start()
    for copy in copies:
        copy.wait_recv()
    for copy in copies:
        copy.wait_send()
    own.wait()


def collect(og):
    anywhere = pl.BlockSpec(memory_space=pl.ANY)
    return pl.pallas_call(
        collect_kernel,
        out_shape=jax.ShapeDtypeStruct((ROW, SLOTS * BLK, GROUP), jnp.bfloat16),
        in_specs=[anywhere],
        out_specs=anywhere,
        scratch_shapes=[
            pltpu.SemaphoreType.DMA((ROW,)), pltpu.SemaphoreType.DMA((ROW,)), pltpu.SemaphoreType.DMA,
        ],
        compiler_params=pltpu.CompilerParams(
            collective_id=2, has_side_effects=True, vmem_limit_bytes=60 << 20
        ),
        name="collect",
    )(og)


def expand_kernel(kept_ref, oc, out, wide, sem):
    c, _, _ = place()
    copies = []
    before = jnp.bool_(False)
    for j in range(TILES_DEV):
        rows = slice(j * BLK, (j + 1) * BLK)
        kept = kept_ref[c * TILES_DEV + j] > 0
        slot = pl.multiple_of(jnp.where(before, BLK, 0), BLK)

        @pl.when(kept)
        def _():
            for h in range(ROW):
                wide[rows, h * GROUP : (h + 1) * GROUP] = oc[h, pl.ds(slot, BLK), :]

        @pl.when(jnp.logical_not(kept))
        def _():
            wide[rows, :] = jnp.zeros((BLK, HEADS * HEAD_DIM), jnp.bfloat16)

        before = before | kept
        copies.append(pltpu.make_async_copy(wide.at[rows], out.at[rows], sem.at[j]))
        copies[-1].start()
    for copy in copies:
        copy.wait()


def expand(kept, oc):
    rows = TILES_DEV * BLK
    return pl.pallas_call(
        expand_kernel,
        out_shape=jax.ShapeDtypeStruct((rows, HEADS * HEAD_DIM), jnp.bfloat16),
        in_specs=[pl.BlockSpec(memory_space=pltpu.SMEM), pl.BlockSpec(memory_space=pltpu.VMEM)],
        out_specs=pl.BlockSpec(memory_space=pl.ANY),
        scratch_shapes=[
            pltpu.VMEM((rows, HEADS * HEAD_DIM), jnp.bfloat16), pltpu.SemaphoreType.DMA((TILES_DEV,)),
        ],
        name="expand",
    )(kept, oc)


def body(queries, key_rows, value_rows, parents, kept_tiles):
    qg, kvg = spread(kept_tiles, queries, key_rows, value_rows)
    og = attend(parents, kept_tiles, qg, kvg)
    return expand(kept_tiles, collect(og))


def solution(mesh):
    return jax.shard_map(
        body,
        mesh=mesh,
        in_specs=(
            P(("dp", "ctx"), None),
            P(("dp", "ctx"), None),
            P(("dp", "ctx"), None),
            P("dp"),
            P("dp"),
        ),
        out_specs=P(("dp", "ctx"), None),
        check_vma=False,
    )
```

```python
import functools

import jax
import jax.numpy as jnp
from jax import lax
from jax.experimental import pallas as pl
from jax.experimental.pallas import tpu as pltpu
from jax.sharding import PartitionSpec as P

HEADS = 16
KV_HEADS = 8
HEAD_DIM = 128
WINDOW = 4096
BLK = 128
TILES_DEV = 4
SLOTS = 2
ROW = 8
BLOCKS = 64
GROUP = 2 * HEAD_DIM
MOST = 18
SIZES = (2, 4, 6, 8, 10, 12, 18)
PAD = MOST - 1
NQ = 3
NEG = -1e30
SCALE = 1.4426950408889634 / 12.0
MESH = pl.DeviceIdType.MESH
STEPS = ((0, 0), (0, 1), (1, 0), (3, 0), (1, 1), (3, 1), (2, 0), (2, 1))
Q_AFTER = 3


def place():
    c = lax.axis_index("ctx")
    return c, c // ROW, c % ROW


def peer(row, r):
    return {"ctx": row * ROW + r}


def ahead(r, step):
    dx, flip = STEPS[step]
    return (r // 2 + dx) % 4 * 2 + (r + flip) % 2


def behind(r, step):
    dx, flip = STEPS[step]
    return (r // 2 + 4 - dx) % 4 * 2 + (r + flip) % 2


def spread_kernel(
    kept_ref, q_hbm, k_hbm, v_hbm, qg, kvg,
    q_v, k_v, v_v, qs, kvs, in_sem, kv_send, kv_recv, q_send, q_recv, up_send, up_recv, own_sem,
):
    c, row, r = place()
    loads = [
        pltpu.make_async_copy(k_hbm, k_v, in_sem.at[0]),
        pltpu.make_async_copy(v_hbm, v_v, in_sem.at[1]),
        pltpu.make_async_copy(q_hbm, q_v, in_sem.at[2]),
    ]
    for load in loads:
        load.start()
    barrier = pltpu.get_barrier_semaphore()
    for step in range(1, ROW):
        pl.semaphore_signal(barrier, 1, device_id=peer(row, (r + step) % ROW), device_id_type=MESH)
    pl.semaphore_signal(barrier, 1, device_id=peer(1 - row, r), device_id_type=MESH)

    f = [kept_ref[c * TILES_DEV + j] > 0 for j in range(TILES_DEV)]

    def pick(ref, slot, cols):
        t = [ref[j * BLK : (j + 1) * BLK, cols] for j in range(TILES_DEV)]
        if slot == 0:
            return jnp.where(f[0], t[0], jnp.where(f[1], t[1], jnp.where(f[2], t[2], t[3])))
        return jnp.where(f[3], t[3], jnp.where(f[2], t[2], jnp.where(f[1], t[1], t[0])))

    def kv_copy(step):
        to = (r + step) % ROW
        return pltpu.make_async_remote_copy(
            kvs.at[to], kvg.at[ROW + r], kv_send.at[step], kv_recv.at[step],
            device_id=peer(row, to), device_id_type=MESH,
        )

    def q_copy(step):
        to = (r + step) % ROW
        return pltpu.make_async_remote_copy(
            qs.at[to], qg.at[r], q_send.at[step], q_recv.at[step],
            device_id=peer(row, to), device_id_type=MESH,
        )

    def up_copy(step):
        s = (r - step + ROW) % ROW
        src = kvs.at[r] if step == 0 else kvg.at[ROW + s]
        return pltpu.make_async_remote_copy(
            src, kvg.at[s], up_send.at[step], up_recv.at[step],
            device_id=peer(1 - row, r), device_id_type=MESH,
        )

    def pack_kv(h):
        cols = pl.ds(pl.multiple_of(h * HEAD_DIM, HEAD_DIM), HEAD_DIM)
        for slot in range(SLOTS):
            kvs[h, slot * BLK : (slot + 1) * BLK, :] = pick(k_v, slot, cols)
            kvs[h, (SLOTS + slot) * BLK : (SLOTS + slot + 1) * BLK, :] = pick(v_v, slot, cols).T

    def pack_q(h):
        for slot in range(SLOTS):
            for g in range(2):
                cols = pl.ds(pl.multiple_of(h * GROUP + g * HEAD_DIM, HEAD_DIM), HEAD_DIM)
                at = slot * 2 * BLK + g * BLK
                qs[h, :, at : at + BLK] = pick(q_v, slot, cols).T

    def kv_copy(step):
        to = ahead(r, step)
        return pltpu.make_async_remote_copy(
            kvs.at[to], kvg.at[ROW + r], kv_send.at[step], kv_recv.at[step],
            device_id=peer(row, to), device_id_type=MESH,
        )

    def q_copy(step):
        to = ahead(r, step)
        return pltpu.make_async_remote_copy(
            qs.at[to], qg.at[r], q_send.at[step], q_recv.at[step],
            device_id=peer(row, to), device_id_type=MESH,
        )

    def up_copy(step):
        s = behind(r, step)
        src = kvs.at[r] if step == 0 else kvg.at[ROW + s]
        return pltpu.make_async_remote_copy(
            src, kvg.at[s], up_send.at[step], up_recv.at[step],
            device_id=peer(1 - row, r), device_id_type=MESH,
        )

    def pass_up(step):
        @pl.when(row == 0)
        def _():
            up_copy(step).start()

    loads[0].wait()
    loads[1].wait()
    pack_kv(r)
    own_kv = pltpu.make_async_copy(kvs.at[r], kvg.at[ROW + r], own_sem.at[0])
    own_kv.start()
    pack_kv(ahead(r, 1))
    pl.semaphore_wait(barrier, ROW)
    pass_up(0)
    for step in range(1, ROW):
        if step > 1:
            pack_kv(ahead(r, step))
        kv_copy(step).start()
    loads[2].wait()
    for step in range(ROW):
        pack_q(ahead(r, step))
    own_q = pltpu.make_async_copy(qs.at[r], qg.at[r], own_sem.at[1])
    own_q.start()
    for step in range(1, ROW):
        kv_copy(step).wait_recv()
        pass_up(step)
        if step == Q_AFTER:
            for other in range(1, ROW):
                q_copy(other).start()
    for step in range(1, ROW):
        q_copy(step).wait_recv()

    @pl.when(row == 1)
    def _():
        for step in range(ROW):
            up_copy(step).wait_recv()

    @pl.when(row == 0)
    def _():
        for step in range(ROW):
            up_copy(step).wait_send()

    for step in range(1, ROW):
        kv_copy(step).wait_send()
        q_copy(step).wait_send()
    own_kv.wait()
    own_q.wait()


def spread(kept, q, k, v):
    rows = q.shape[0]
    anywhere = pl.BlockSpec(memory_space=pl.ANY)
    bf16 = jnp.bfloat16
    dma = pltpu.SemaphoreType.DMA
    return pl.pallas_call(
        spread_kernel,
        out_shape=(
            jax.ShapeDtypeStruct((ROW, HEAD_DIM, SLOTS * 2 * BLK), bf16),
            jax.ShapeDtypeStruct((2 * ROW, 2 * SLOTS * BLK, HEAD_DIM), bf16),
        ),
        in_specs=[pl.BlockSpec(memory_space=pltpu.SMEM), anywhere, anywhere, anywhere],
        out_specs=(anywhere, anywhere),
        scratch_shapes=[
            pltpu.VMEM((rows, HEADS * HEAD_DIM), bf16),
            pltpu.VMEM((rows, KV_HEADS * HEAD_DIM), bf16),
            pltpu.VMEM((rows, KV_HEADS * HEAD_DIM), bf16),
            pltpu.VMEM((ROW, HEAD_DIM, SLOTS * 2 * BLK), bf16),
            pltpu.VMEM((ROW, 2 * SLOTS * BLK, HEAD_DIM), bf16),
            dma((3,)), dma((ROW,)), dma((ROW,)), dma((ROW,)), dma((ROW,)), dma((ROW,)), dma((ROW,)), dma((2,)),
        ],
        compiler_params=pltpu.CompilerParams(
            collective_id=1, has_side_effects=True, vmem_limit_bytes=60 << 20
        ),
        name="spread",
    )(kept, q, k, v)


def attend_kernel(
    parents_ref, kept_ref, qg, kvg, og,
    q_v, kv_v, o_v, bias_ref, up_ref, base_ref, list_ref, seen_ref, size_ref, in_sem, out_sem,
):
    c, row, r = place()
    half = ROW * 2 * SLOTS * BLK
    load_own = pltpu.make_async_copy(kvg.at[half:], kv_v.at[half:], in_sem.at[0])
    load_low = pltpu.make_async_copy(kvg.at[:half], kv_v.at[:half], in_sem.at[1])
    load_q = pltpu.make_async_copy(qg, q_v, in_sem.at[2])
    load_q.start()
    load_own.start()

    @pl.when(row == 1)
    def _():
        load_low.start()

    end = BLOCKS
    reach = WINDOW // BLK
    first_tile = row * ROW * TILES_DEV

    up_ref[end] = -BLOCKS * 4
    up_ref[0] = end
    for t in range(1, BLOCKS):
        p = parents_ref[t]
        up_ref[t] = jnp.where(kept_ref[p] > 0, p, up_ref[p])
    base_ref[end] = half
    for s in range(BLOCKS // TILES_DEV):
        lin = jnp.clip(s - ROW * row + ROW, 0, 2 * ROW - 1) * (2 * SLOTS * BLK)
        before = jnp.int32(0)
        for j in range(TILES_DEV):
            t = s * TILES_DEV + j
            base_ref[t] = lin + jnp.minimum(before, SLOTS - 1) * BLK
            before = before + jnp.where(kept_ref[t] > 0, 1, 0)
    count = jnp.int32(0)
    for j in range(ROW * TILES_DEV):
        t = first_tile + j
        list_ref[count] = t
        count = count + jnp.where(kept_ref[t] > 0, 1, 0)

    def gather(i, _):
        t = list_ref[i]

        def visit(state):
            node, k = state
            seen_ref[i * MOST + k] = base_ref[node] + jnp.where(t - node == reach, 2, 0)
            nxt = up_ref[node]
            return jnp.where(nxt >= t - reach, nxt, end), k + 1

        _, k = lax.while_loop(lambda state: state[0] < end, visit, (t, jnp.int32(0)))
        size_ref[i] = k
        for extra in range(PAD):
            seen_ref[i * MOST + k + extra] = base_ref[end] + 1
        return 0

    lax.fori_loop(0, count, gather, 0)
    rc = lax.broadcasted_iota(jnp.int32, (BLK, BLK), 1) - lax.broadcasted_iota(jnp.int32, (BLK, BLK), 0)
    bias_ref[0] = jnp.zeros((BLK, BLK), jnp.float32)
    bias_ref[1] = jnp.full((BLK, BLK), NEG, jnp.float32)
    bias_ref[2] = jnp.where(rc < 0, 0.0, NEG)
    bias_ref[3] = jnp.where(rc >= 0, 0.0, NEG)
    load_q.wait()
    load_own.wait()

    @pl.when(row == 1)
    def _():
        load_low.wait()

    def some(j, _):
        which = [jnp.minimum(NQ * j + n, count - 1) for n in range(NQ)]
        spots, heads = [], []
        for i in which:
            t = list_ref[i]
            slot = (base_ref[t] // BLK) % SLOTS
            shard = (t - first_tile) // TILES_DEV
            spots.append((shard, pl.multiple_of(slot * BLK, BLK)))
            heads.append(q_v[shard, :, pl.ds(pl.multiple_of(slot * 2 * BLK, 2 * BLK), 2 * BLK)])
        longest = functools.reduce(jnp.maximum, [size_ref[i] for i in which])

        def over(size):
            parts = [[] for _ in which]
            tops = [None for _ in which]
            values = [[] for _ in which]
            for n, i in enumerate(which):
                for g in range(size):
                    entry = seen_ref[i * MOST + g]
                    base = pl.multiple_of(entry // BLK * BLK, BLK)
                    bias = bias_ref[3 if g == 0 else entry % BLK]
                    s = jnp.dot(kv_v[pl.ds(base, BLK), :], heads[n], preferred_element_type=jnp.float32) * SCALE
                    s = s + jnp.concatenate([bias, bias], 1)
                    fold = jnp.max(s.reshape(BLK // 8, 8, 2 * BLK), axis=0)
                    tops[n] = fold if g == 0 else jnp.maximum(tops[n], fold)
                    parts[n].append(s)
                    values[n].append(kv_v[pl.ds(base + SLOTS * BLK, BLK), :])
            tops = [jnp.max(top, axis=0, keepdims=True) for top in tops]
            accs, totals = [], []
            for n in range(NQ):
                weights, total = [], None
                for part in parts[n]:
                    term = jnp.exp2(part - tops[n])
                    fold = jnp.sum(term.reshape(BLK // 8, 8, 2 * BLK), axis=0)
                    total = fold if total is None else total + fold
                    weights.append(term.astype(jnp.bfloat16))
                totals.append(jnp.sum(total, axis=0, keepdims=True))
                w = jnp.concatenate(weights, 0)
                accs.append(jnp.dot(jnp.concatenate(values[n], 1), w, preferred_element_type=jnp.float32))
            outs = [(acc / total).astype(jnp.bfloat16) for acc, total in zip(accs, totals)]
            outs = [jnp.concatenate([o[:, :BLK].T, o[:, BLK:].T], 1) for o in outs]
            for i, o in zip(which, outs):
                o_v[i] = o

        for low, size in zip((0, *SIZES), SIZES):
            pl.when((longest > low) & (longest <= size))(functools.partial(over, size))
        for n in range(NQ):

            @pl.when(NQ * j + n < count)
            def _():
                shard, at = spots[n]
                pltpu.make_async_copy(
                    o_v.at[which[n]], og.at[shard, pl.ds(at, BLK), :], out_sem.at[which[n]]
                ).start()

        return 0

    lax.fori_loop(0, (count + NQ - 1) // NQ, some, 0)

    def drain(w, _):
        pltpu.make_async_copy(o_v.at[w], og.at[0, pl.ds(0, BLK), :], out_sem.at[w]).wait()
        return 0

    lax.fori_loop(0, count, drain, 0)


def attend(parents, kept, qg, kvg):
    smem = pl.BlockSpec(memory_space=pltpu.SMEM)
    anywhere = pl.BlockSpec(memory_space=pl.ANY)
    bf16 = jnp.bfloat16
    rows = 2 * ROW * 2 * SLOTS * BLK
    return pl.pallas_call(
        attend_kernel,
        out_shape=jax.ShapeDtypeStruct((ROW, SLOTS * BLK, GROUP), bf16),
        in_specs=[smem, smem, anywhere, anywhere],
        out_specs=anywhere,
        scratch_shapes=[
            pltpu.VMEM((ROW, HEAD_DIM, SLOTS * 2 * BLK), bf16),
            pltpu.VMEM((rows, HEAD_DIM), bf16),
            pltpu.VMEM((ROW * SLOTS, BLK, GROUP), bf16),
            pltpu.VMEM((4, BLK, BLK), jnp.float32),
            pltpu.SMEM((BLOCKS + 1,), jnp.int32),
            pltpu.SMEM((BLOCKS + 1,), jnp.int32),
            pltpu.SMEM((ROW * TILES_DEV + 1,), jnp.int32),
            pltpu.SMEM((ROW * SLOTS * MOST + PAD,), jnp.int32),
            pltpu.SMEM((ROW * SLOTS,), jnp.int32),
            pltpu.SemaphoreType.DMA((3,)),
            pltpu.SemaphoreType.DMA((ROW * SLOTS,)),
        ],
        compiler_params=pltpu.CompilerParams(vmem_limit_bytes=60 << 20),
        name="attend",
    )(parents, kept, qg, kvg.reshape(rows, HEAD_DIM))


def collect_kernel(og, oc, send, recv, own_sem):
    _, row, r = place()
    barrier = pltpu.get_barrier_semaphore()
    for step in range(1, ROW):
        pl.semaphore_signal(barrier, 1, device_id=peer(row, (r + step) % ROW), device_id_type=MESH)
    own = pltpu.make_async_copy(og.at[r], oc.at[r], own_sem)
    own.start()
    pl.semaphore_wait(barrier, ROW - 1)
    copies = []
    for step in range(1, ROW):
        to = (r + step) % ROW
        copies.append(
            pltpu.make_async_remote_copy(
                og.at[to], oc.at[r], send.at[step], recv.at[step],
                device_id=peer(row, to), device_id_type=MESH,
            )
        )
    for copy in copies:
        copy.start()
    for copy in copies:
        copy.wait_recv()
    for copy in copies:
        copy.wait_send()
    own.wait()


def collect(og):
    anywhere = pl.BlockSpec(memory_space=pl.ANY)
    return pl.pallas_call(
        collect_kernel,
        out_shape=jax.ShapeDtypeStruct((ROW, SLOTS * BLK, GROUP), jnp.bfloat16),
        in_specs=[anywhere],
        out_specs=anywhere,
        scratch_shapes=[
            pltpu.SemaphoreType.DMA((ROW,)), pltpu.SemaphoreType.DMA((ROW,)), pltpu.SemaphoreType.DMA,
        ],
        compiler_params=pltpu.CompilerParams(
            collective_id=2, has_side_effects=True, vmem_limit_bytes=60 << 20
        ),
        name="collect",
    )(og)


def expand_kernel(kept_ref, oc, out, wide, sem):
    c, _, _ = place()
    copies = []
    before = jnp.bool_(False)
    for j in range(TILES_DEV):
        rows = slice(j * BLK, (j + 1) * BLK)
        kept = kept_ref[c * TILES_DEV + j] > 0
        slot = pl.multiple_of(jnp.where(before, BLK, 0), BLK)

        @pl.when(kept)
        def _():
            for h in range(ROW):
                wide[rows, h * GROUP : (h + 1) * GROUP] = oc[h, pl.ds(slot, BLK), :]

        @pl.when(jnp.logical_not(kept))
        def _():
            wide[rows, :] = jnp.zeros((BLK, HEADS * HEAD_DIM), jnp.bfloat16)

        before = before | kept
        copies.append(pltpu.make_async_copy(wide.at[rows], out.at[rows], sem.at[j]))
        copies[-1].start()
    for copy in copies:
        copy.wait()


def expand(kept, oc):
    rows = TILES_DEV * BLK
    return pl.pallas_call(
        expand_kernel,
        out_shape=jax.ShapeDtypeStruct((rows, HEADS * HEAD_DIM), jnp.bfloat16),
        in_specs=[pl.BlockSpec(memory_space=pltpu.SMEM), pl.BlockSpec(memory_space=pltpu.VMEM)],
        out_specs=pl.BlockSpec(memory_space=pl.ANY),
        scratch_shapes=[
            pltpu.VMEM((rows, HEADS * HEAD_DIM), jnp.bfloat16), pltpu.SemaphoreType.DMA((TILES_DEV,)),
        ],
        name="expand",
    )(kept, oc)


def body(queries, key_rows, value_rows, parents, kept_tiles):
    qg, kvg = spread(kept_tiles, queries, key_rows, value_rows)
    og = attend(parents, kept_tiles, qg, kvg)
    return expand(kept_tiles, collect(og))


def solution(mesh):
    return jax.shard_map(
        body,
        mesh=mesh,
        in_specs=(
            P(("dp", "ctx"), None),
            P(("dp", "ctx"), None),
            P(("dp", "ctx"), None),
            P("dp"),
            P("dp"),
        ),
        out_specs=P(("dp", "ctx"), None),
        check_vma=False,
    )
```

```python
import functools

import jax
import jax.numpy as jnp
from jax import lax
from jax.experimental import pallas as pl
from jax.experimental.pallas import tpu as pltpu
from jax.sharding import PartitionSpec as P

HEADS = 16
KV_HEADS = 8
HEAD_DIM = 128
WINDOW = 4096
BLK = 128
TILES_DEV = 4
SLOTS = 2
ROW = 8
BLOCKS = 64
GROUP = 2 * HEAD_DIM
MOST = 18
SIZES = (2, 4, 6, 8, 10, 12, 18)
PAD = MOST - 1
WIDE = 4
NARROW = 2
NEG = -1e30
SCALE = 1.4426950408889634 / 12.0
MESH = pl.DeviceIdType.MESH
STEPS = ((0, 0), (0, 1), (1, 0), (3, 0), (1, 1), (3, 1), (2, 0), (2, 1))
Q_AFTER = 3


def place():
    c = lax.axis_index("ctx")
    return c, c // ROW, c % ROW


def peer(row, r):
    return {"ctx": row * ROW + r}


def ahead(r, step):
    dx, flip = STEPS[step]
    return (r // 2 + dx) % 4 * 2 + (r + flip) % 2


def behind(r, step):
    dx, flip = STEPS[step]
    return (r // 2 + 4 - dx) % 4 * 2 + (r + flip) % 2


def spread_kernel(
    kept_ref, q_hbm, k_hbm, v_hbm, qg, kvg,
    q_v, k_v, v_v, qs, kvs, in_sem, kv_send, kv_recv, q_send, q_recv, up_send, up_recv, own_sem,
):
    c, row, r = place()
    loads = [
        pltpu.make_async_copy(k_hbm, k_v, in_sem.at[0]),
        pltpu.make_async_copy(v_hbm, v_v, in_sem.at[1]),
        pltpu.make_async_copy(q_hbm, q_v, in_sem.at[2]),
    ]
    for load in loads:
        load.start()
    barrier = pltpu.get_barrier_semaphore()
    for step in range(1, ROW):
        pl.semaphore_signal(barrier, 1, device_id=peer(row, (r + step) % ROW), device_id_type=MESH)
    pl.semaphore_signal(barrier, 1, device_id=peer(1 - row, r), device_id_type=MESH)

    f = [kept_ref[c * TILES_DEV + j] > 0 for j in range(TILES_DEV)]

    def pick(ref, slot, cols):
        t = [ref[j * BLK : (j + 1) * BLK, cols] for j in range(TILES_DEV)]
        if slot == 0:
            return jnp.where(f[0], t[0], jnp.where(f[1], t[1], jnp.where(f[2], t[2], t[3])))
        return jnp.where(f[3], t[3], jnp.where(f[2], t[2], jnp.where(f[1], t[1], t[0])))

    def kv_copy(step):
        to = (r + step) % ROW
        return pltpu.make_async_remote_copy(
            kvs.at[to], kvg.at[ROW + r], kv_send.at[step], kv_recv.at[step],
            device_id=peer(row, to), device_id_type=MESH,
        )

    def q_copy(step):
        to = (r + step) % ROW
        return pltpu.make_async_remote_copy(
            qs.at[to], qg.at[r], q_send.at[step], q_recv.at[step],
            device_id=peer(row, to), device_id_type=MESH,
        )

    def up_copy(step):
        s = (r - step + ROW) % ROW
        src = kvs.at[r] if step == 0 else kvg.at[ROW + s]
        return pltpu.make_async_remote_copy(
            src, kvg.at[s], up_send.at[step], up_recv.at[step],
            device_id=peer(1 - row, r), device_id_type=MESH,
        )

    def pack_kv(h):
        cols = pl.ds(pl.multiple_of(h * HEAD_DIM, HEAD_DIM), HEAD_DIM)
        for slot in range(SLOTS):
            kvs[h, slot * BLK : (slot + 1) * BLK, :] = pick(k_v, slot, cols)
            kvs[h, (SLOTS + slot) * BLK : (SLOTS + slot + 1) * BLK, :] = pick(v_v, slot, cols).T

    def pack_q(h):
        for slot in range(SLOTS):
            for g in range(2):
                cols = pl.ds(pl.multiple_of(h * GROUP + g * HEAD_DIM, HEAD_DIM), HEAD_DIM)
                at = slot * 2 * BLK + g * BLK
                qs[h, :, at : at + BLK] = pick(q_v, slot, cols).T

    def kv_copy(step):
        to = ahead(r, step)
        return pltpu.make_async_remote_copy(
            kvs.at[to], kvg.at[ROW + r], kv_send.at[step], kv_recv.at[step],
            device_id=peer(row, to), device_id_type=MESH,
        )

    def q_copy(step):
        to = ahead(r, step)
        return pltpu.make_async_remote_copy(
            qs.at[to], qg.at[r], q_send.at[step], q_recv.at[step],
            device_id=peer(row, to), device_id_type=MESH,
        )

    def up_copy(step):
        s = behind(r, step)
        src = kvs.at[r] if step == 0 else kvg.at[ROW + s]
        return pltpu.make_async_remote_copy(
            src, kvg.at[s], up_send.at[step], up_recv.at[step],
            device_id=peer(1 - row, r), device_id_type=MESH,
        )

    def pass_up(step):
        @pl.when(row == 0)
        def _():
            up_copy(step).start()

    loads[0].wait()
    loads[1].wait()
    pack_kv(r)
    own_kv = pltpu.make_async_copy(kvs.at[r], kvg.at[ROW + r], own_sem.at[0])
    own_kv.start()
    pack_kv(ahead(r, 1))
    pl.semaphore_wait(barrier, ROW)
    pass_up(0)
    for step in range(1, ROW):
        if step > 1:
            pack_kv(ahead(r, step))
        kv_copy(step).start()
    loads[2].wait()
    for step in range(ROW):
        pack_q(ahead(r, step))
    own_q = pltpu.make_async_copy(qs.at[r], qg.at[r], own_sem.at[1])
    own_q.start()
    for step in range(1, ROW):
        kv_copy(step).wait_recv()
        pass_up(step)
        if step == Q_AFTER:
            for other in range(1, ROW):
                q_copy(other).start()
    for step in range(1, ROW):
        q_copy(step).wait_recv()

    @pl.when(row == 1)
    def _():
        for step in range(ROW):
            up_copy(step).wait_recv()

    @pl.when(row == 0)
    def _():
        for step in range(ROW):
            up_copy(step).wait_send()

    for step in range(1, ROW):
        kv_copy(step).wait_send()
        q_copy(step).wait_send()
    own_kv.wait()
    own_q.wait()


def spread(kept, q, k, v):
    rows = q.shape[0]
    anywhere = pl.BlockSpec(memory_space=pl.ANY)
    bf16 = jnp.bfloat16
    dma = pltpu.SemaphoreType.DMA
    return pl.pallas_call(
        spread_kernel,
        out_shape=(
            jax.ShapeDtypeStruct((ROW, HEAD_DIM, SLOTS * 2 * BLK), bf16),
            jax.ShapeDtypeStruct((2 * ROW, 2 * SLOTS * BLK, HEAD_DIM), bf16),
        ),
        in_specs=[pl.BlockSpec(memory_space=pltpu.SMEM), anywhere, anywhere, anywhere],
        out_specs=(anywhere, anywhere),
        scratch_shapes=[
            pltpu.VMEM((rows, HEADS * HEAD_DIM), bf16),
            pltpu.VMEM((rows, KV_HEADS * HEAD_DIM), bf16),
            pltpu.VMEM((rows, KV_HEADS * HEAD_DIM), bf16),
            pltpu.VMEM((ROW, HEAD_DIM, SLOTS * 2 * BLK), bf16),
            pltpu.VMEM((ROW, 2 * SLOTS * BLK, HEAD_DIM), bf16),
            dma((3,)), dma((ROW,)), dma((ROW,)), dma((ROW,)), dma((ROW,)), dma((ROW,)), dma((ROW,)), dma((2,)),
        ],
        compiler_params=pltpu.CompilerParams(
            collective_id=1, has_side_effects=True, vmem_limit_bytes=60 << 20
        ),
        name="spread",
    )(kept, q, k, v)


def attend_kernel(
    parents_ref, kept_ref, qg, kvg, og,
    q_v, kv_v, o_v, bias_ref, up_ref, base_ref, list_ref, seen_ref, size_ref, in_sem, out_sem,
):
    c, row, r = place()
    half = ROW * 2 * SLOTS * BLK
    load_own = pltpu.make_async_copy(kvg.at[half:], kv_v.at[half:], in_sem.at[0])
    load_low = pltpu.make_async_copy(kvg.at[:half], kv_v.at[:half], in_sem.at[1])
    load_q = pltpu.make_async_copy(qg, q_v, in_sem.at[2])
    load_q.start()
    load_own.start()

    @pl.when(row == 1)
    def _():
        load_low.start()

    end = BLOCKS
    reach = WINDOW // BLK
    first_tile = row * ROW * TILES_DEV

    up_ref[end] = -BLOCKS * 4
    up_ref[0] = end
    for t in range(1, BLOCKS):
        p = parents_ref[t]
        up_ref[t] = jnp.where(kept_ref[p] > 0, p, up_ref[p])
    base_ref[end] = half
    for s in range(BLOCKS // TILES_DEV):
        lin = jnp.clip(s - ROW * row + ROW, 0, 2 * ROW - 1) * (2 * SLOTS * BLK)
        before = jnp.int32(0)
        for j in range(TILES_DEV):
            t = s * TILES_DEV + j
            base_ref[t] = lin + jnp.minimum(before, SLOTS - 1) * BLK
            before = before + jnp.where(kept_ref[t] > 0, 1, 0)
    count = jnp.int32(0)
    for j in range(ROW * TILES_DEV):
        t = first_tile + j
        list_ref[count] = t
        count = count + jnp.where(kept_ref[t] > 0, 1, 0)

    def gather(i, _):
        t = list_ref[i]

        def visit(state):
            node, k = state
            seen_ref[i * MOST + k] = base_ref[node] + jnp.where(t - node == reach, 2, 0)
            nxt = up_ref[node]
            return jnp.where(nxt >= t - reach, nxt, end), k + 1

        _, k = lax.while_loop(lambda state: state[0] < end, visit, (t, jnp.int32(0)))
        size_ref[i] = k
        for extra in range(PAD):
            seen_ref[i * MOST + k + extra] = base_ref[end] + 1
        return 0

    lax.fori_loop(0, count, gather, 0)
    rc = lax.broadcasted_iota(jnp.int32, (BLK, BLK), 1) - lax.broadcasted_iota(jnp.int32, (BLK, BLK), 0)
    bias_ref[0] = jnp.zeros((BLK, BLK), jnp.float32)
    bias_ref[1] = jnp.full((BLK, BLK), NEG, jnp.float32)
    bias_ref[2] = jnp.where(rc < 0, 0.0, NEG)
    bias_ref[3] = jnp.where(rc >= 0, 0.0, NEG)
    load_q.wait()
    load_own.wait()

    @pl.when(row == 1)
    def _():
        load_low.wait()

    def some(width, first, j, _):
        which = [jnp.minimum(first + width * j + n, count - 1) for n in range(width)]
        spots, heads = [], []
        for i in which:
            t = list_ref[i]
            slot = (base_ref[t] // BLK) % SLOTS
            shard = (t - first_tile) // TILES_DEV
            spots.append((shard, pl.multiple_of(slot * BLK, BLK)))
            heads.append(q_v[shard, :, pl.ds(pl.multiple_of(slot * 2 * BLK, 2 * BLK), 2 * BLK)])
        longest = functools.reduce(jnp.maximum, [size_ref[i] for i in which])

        def over(size):
            parts = [[] for _ in which]
            tops = [None for _ in which]
            values = [[] for _ in which]
            for n, i in enumerate(which):
                for g in range(size):
                    entry = seen_ref[i * MOST + g]
                    base = pl.multiple_of(entry // BLK * BLK, BLK)
                    bias = bias_ref[3 if g == 0 else entry % BLK]
                    s = jnp.dot(kv_v[pl.ds(base, BLK), :], heads[n], preferred_element_type=jnp.float32) * SCALE
                    s = s + jnp.concatenate([bias, bias], 1)
                    fold = jnp.max(s.reshape(BLK // 8, 8, 2 * BLK), axis=0)
                    tops[n] = fold if g == 0 else jnp.maximum(tops[n], fold)
                    parts[n].append(s)
                    values[n].append(kv_v[pl.ds(base + SLOTS * BLK, BLK), :])
            tops = [jnp.max(top, axis=0, keepdims=True) for top in tops]
            accs, totals = [], []
            for n in range(width):
                weights, total = [], None
                for part in parts[n]:
                    term = jnp.exp2(part - tops[n])
                    fold = jnp.sum(term.reshape(BLK // 8, 8, 2 * BLK), axis=0)
                    total = fold if total is None else total + fold
                    weights.append(term.astype(jnp.bfloat16))
                totals.append(jnp.sum(total, axis=0, keepdims=True))
                w = jnp.concatenate(weights, 0)
                accs.append(jnp.dot(jnp.concatenate(values[n], 1), w, preferred_element_type=jnp.float32))
            outs = [(acc / total).astype(jnp.bfloat16) for acc, total in zip(accs, totals)]
            outs = [jnp.concatenate([o[:, :BLK].T, o[:, BLK:].T], 1) for o in outs]
            for i, o in zip(which, outs):
                o_v[i] = o

        for low, size in zip((0, *SIZES), SIZES):
            pl.when((longest > low) & (longest <= size))(functools.partial(over, size))
        for n in range(width):

            @pl.when(first + width * j + n < count)
            def _():
                shard, at = spots[n]
                pltpu.make_async_copy(
                    o_v.at[which[n]], og.at[shard, pl.ds(at, BLK), :], out_sem.at[which[n]]
                ).start()

        return 0

    many = count // WIDE
    lax.fori_loop(0, many, functools.partial(some, WIDE, 0), 0)
    left = count - WIDE * many
    lax.fori_loop(0, (left + NARROW - 1) // NARROW, functools.partial(some, NARROW, WIDE * many), 0)

    def drain(w, _):
        pltpu.make_async_copy(o_v.at[w], og.at[0, pl.ds(0, BLK), :], out_sem.at[w]).wait()
        return 0

    lax.fori_loop(0, count, drain, 0)


def attend(parents, kept, qg, kvg):
    smem = pl.BlockSpec(memory_space=pltpu.SMEM)
    anywhere = pl.BlockSpec(memory_space=pl.ANY)
    bf16 = jnp.bfloat16
    rows = 2 * ROW * 2 * SLOTS * BLK
    return pl.pallas_call(
        attend_kernel,
        out_shape=jax.ShapeDtypeStruct((ROW, SLOTS * BLK, GROUP), bf16),
        in_specs=[smem, smem, anywhere, anywhere],
        out_specs=anywhere,
        scratch_shapes=[
            pltpu.VMEM((ROW, HEAD_DIM, SLOTS * 2 * BLK), bf16),
            pltpu.VMEM((rows, HEAD_DIM), bf16),
            pltpu.VMEM((ROW * SLOTS, BLK, GROUP), bf16),
            pltpu.VMEM((4, BLK, BLK), jnp.float32),
            pltpu.SMEM((BLOCKS + 1,), jnp.int32),
            pltpu.SMEM((BLOCKS + 1,), jnp.int32),
            pltpu.SMEM((ROW * TILES_DEV + 1,), jnp.int32),
            pltpu.SMEM((ROW * SLOTS * MOST + PAD,), jnp.int32),
            pltpu.SMEM((ROW * SLOTS,), jnp.int32),
            pltpu.SemaphoreType.DMA((3,)),
            pltpu.SemaphoreType.DMA((ROW * SLOTS,)),
        ],
        compiler_params=pltpu.CompilerParams(vmem_limit_bytes=60 << 20),
        name="attend",
    )(parents, kept, qg, kvg.reshape(rows, HEAD_DIM))


def collect_kernel(og, oc, send, recv, own_sem):
    _, row, r = place()
    barrier = pltpu.get_barrier_semaphore()
    for step in range(1, ROW):
        pl.semaphore_signal(barrier, 1, device_id=peer(row, (r + step) % ROW), device_id_type=MESH)
    own = pltpu.make_async_copy(og.at[r], oc.at[r], own_sem)
    own.start()
    pl.semaphore_wait(barrier, ROW - 1)
    copies = []
    for step in range(1, ROW):
        to = (r + step) % ROW
        copies.append(
            pltpu.make_async_remote_copy(
                og.at[to], oc.at[r], send.at[step], recv.at[step],
                device_id=peer(row, to), device_id_type=MESH,
            )
        )
    for copy in copies:
        copy.start()
    for copy in copies:
        copy.wait_recv()
    for copy in copies:
        copy.wait_send()
    own.wait()


def collect(og):
    anywhere = pl.BlockSpec(memory_space=pl.ANY)
    return pl.pallas_call(
        collect_kernel,
        out_shape=jax.ShapeDtypeStruct((ROW, SLOTS * BLK, GROUP), jnp.bfloat16),
        in_specs=[anywhere],
        out_specs=anywhere,
        scratch_shapes=[
            pltpu.SemaphoreType.DMA((ROW,)), pltpu.SemaphoreType.DMA((ROW,)), pltpu.SemaphoreType.DMA,
        ],
        compiler_params=pltpu.CompilerParams(
            collective_id=2, has_side_effects=True, vmem_limit_bytes=60 << 20
        ),
        name="collect",
    )(og)


def expand_kernel(kept_ref, oc, out, wide, sem):
    c, _, _ = place()
    copies = []
    before = jnp.bool_(False)
    for j in range(TILES_DEV):
        rows = slice(j * BLK, (j + 1) * BLK)
        kept = kept_ref[c * TILES_DEV + j] > 0
        slot = pl.multiple_of(jnp.where(before, BLK, 0), BLK)

        @pl.when(kept)
        def _():
            for h in range(ROW):
                wide[rows, h * GROUP : (h + 1) * GROUP] = oc[h, pl.ds(slot, BLK), :]

        @pl.when(jnp.logical_not(kept))
        def _():
            wide[rows, :] = jnp.zeros((BLK, HEADS * HEAD_DIM), jnp.bfloat16)

        before = before | kept
        copies.append(pltpu.make_async_copy(wide.at[rows], out.at[rows], sem.at[j]))
        copies[-1].start()
    for copy in copies:
        copy.wait()


def expand(kept, oc):
    rows = TILES_DEV * BLK
    return pl.pallas_call(
        expand_kernel,
        out_shape=jax.ShapeDtypeStruct((rows, HEADS * HEAD_DIM), jnp.bfloat16),
        in_specs=[pl.BlockSpec(memory_space=pltpu.SMEM), pl.BlockSpec(memory_space=pltpu.VMEM)],
        out_specs=pl.BlockSpec(memory_space=pl.ANY),
        scratch_shapes=[
            pltpu.VMEM((rows, HEADS * HEAD_DIM), jnp.bfloat16), pltpu.SemaphoreType.DMA((TILES_DEV,)),
        ],
        name="expand",
    )(kept, oc)


def body(queries, key_rows, value_rows, parents, kept_tiles):
    qg, kvg = spread(kept_tiles, queries, key_rows, value_rows)
    og = attend(parents, kept_tiles, qg, kvg)
    return expand(kept_tiles, collect(og))


def solution(mesh):
    return jax.shard_map(
        body,
        mesh=mesh,
        in_specs=(
            P(("dp", "ctx"), None),
            P(("dp", "ctx"), None),
            P(("dp", "ctx"), None),
            P("dp"),
            P("dp"),
        ),
        out_specs=P(("dp", "ctx"), None),
        check_vma=False,
    )
```

```python
import functools

import jax
import jax.numpy as jnp
from jax import lax
from jax.experimental import pallas as pl
from jax.experimental.pallas import tpu as pltpu
from jax.sharding import PartitionSpec as P

HEADS = 16
KV_HEADS = 8
HEAD_DIM = 128
WINDOW = 4096
BLK = 128
TILES_DEV = 4
SLOTS = 2
ROW = 8
BLOCKS = 64
GROUP = 2 * HEAD_DIM
MOST = 18
SIZES = (2, 4, 6, 8, 10, 12, 18)
PAD = MOST - 1
WIDE = 4
NARROW = 2
NEG = -1e30
SCALE = 1.4426950408889634 / 12.0
MESH = pl.DeviceIdType.MESH
STEPS = ((0, 0), (0, 1), (1, 0), (3, 0), (1, 1), (3, 1), (2, 0), (2, 1))
Q_AFTER = 3


def place():
    c = lax.axis_index("ctx")
    return c, c // ROW, c % ROW


def peer(row, r):
    return {"ctx": row * ROW + r}


def ahead(r, step):
    dx, flip = STEPS[step]
    return (r // 2 + dx) % 4 * 2 + (r + flip) % 2


def behind(r, step):
    dx, flip = STEPS[step]
    return (r // 2 + 4 - dx) % 4 * 2 + (r + flip) % 2


def spread_kernel(
    kept_ref, q_hbm, k_hbm, v_hbm, qg, kvg,
    q_v, k_v, v_v, qs, kvs, in_sem, kv_send, kv_recv, q_send, q_recv, up_send, up_recv, own_sem,
):
    c, row, r = place()
    loads = [
        pltpu.make_async_copy(k_hbm, k_v, in_sem.at[0]),
        pltpu.make_async_copy(v_hbm, v_v, in_sem.at[1]),
        pltpu.make_async_copy(q_hbm, q_v, in_sem.at[2]),
    ]
    for load in loads:
        load.start()
    barrier = pltpu.get_barrier_semaphore()
    for step in range(1, ROW):
        pl.semaphore_signal(barrier, 1, device_id=peer(row, (r + step) % ROW), device_id_type=MESH)
    pl.semaphore_signal(barrier, 1, device_id=peer(1 - row, r), device_id_type=MESH)

    f = [kept_ref[c * TILES_DEV + j] > 0 for j in range(TILES_DEV)]

    def pick(ref, slot, cols):
        t = [ref[j * BLK : (j + 1) * BLK, cols] for j in range(TILES_DEV)]
        if slot == 0:
            return jnp.where(f[0], t[0], jnp.where(f[1], t[1], jnp.where(f[2], t[2], t[3])))
        return jnp.where(f[3], t[3], jnp.where(f[2], t[2], jnp.where(f[1], t[1], t[0])))

    def kv_copy(step):
        to = (r + step) % ROW
        return pltpu.make_async_remote_copy(
            kvs.at[to], kvg.at[ROW + r], kv_send.at[step], kv_recv.at[step],
            device_id=peer(row, to), device_id_type=MESH,
        )

    def q_copy(step):
        to = (r + step) % ROW
        return pltpu.make_async_remote_copy(
            qs.at[to], qg.at[r], q_send.at[step], q_recv.at[step],
            device_id=peer(row, to), device_id_type=MESH,
        )

    def up_copy(step):
        s = (r - step + ROW) % ROW
        src = kvs.at[r] if step == 0 else kvg.at[ROW + s]
        return pltpu.make_async_remote_copy(
            src, kvg.at[s], up_send.at[step], up_recv.at[step],
            device_id=peer(1 - row, r), device_id_type=MESH,
        )

    def pack_kv(h):
        cols = pl.ds(pl.multiple_of(h * HEAD_DIM, HEAD_DIM), HEAD_DIM)
        for slot in range(SLOTS):
            kvs[h, slot * BLK : (slot + 1) * BLK, :] = pick(k_v, slot, cols)
            kvs[h, (SLOTS + slot) * BLK : (SLOTS + slot + 1) * BLK, :] = pick(v_v, slot, cols).T

    def pack_q(h):
        for slot in range(SLOTS):
            for g in range(2):
                cols = pl.ds(pl.multiple_of(h * GROUP + g * HEAD_DIM, HEAD_DIM), HEAD_DIM)
                at = slot * 2 * BLK + g * BLK
                qs[h, :, at : at + BLK] = pick(q_v, slot, cols).T

    def kv_copy(step):
        to = ahead(r, step)
        return pltpu.make_async_remote_copy(
            kvs.at[to], kvg.at[ROW + r], kv_send.at[step], kv_recv.at[step],
            device_id=peer(row, to), device_id_type=MESH,
        )

    def q_copy(step):
        to = ahead(r, step)
        return pltpu.make_async_remote_copy(
            qs.at[to], qg.at[r], q_send.at[step], q_recv.at[step],
            device_id=peer(row, to), device_id_type=MESH,
        )

    def up_copy(step):
        s = behind(r, step)
        src = kvs.at[r] if step == 0 else kvg.at[ROW + s]
        return pltpu.make_async_remote_copy(
            src, kvg.at[s], up_send.at[step], up_recv.at[step],
            device_id=peer(1 - row, r), device_id_type=MESH,
        )

    def pass_up(step):
        @pl.when(row == 0)
        def _():
            up_copy(step).start()

    loads[0].wait()
    loads[1].wait()
    pack_kv(r)
    own_kv = pltpu.make_async_copy(kvs.at[r], kvg.at[ROW + r], own_sem.at[0])
    own_kv.start()
    pack_kv(ahead(r, 1))
    pl.semaphore_wait(barrier, ROW)
    pass_up(0)
    for step in range(1, ROW):
        if step > 1:
            pack_kv(ahead(r, step))
        kv_copy(step).start()
    loads[2].wait()
    for step in range(ROW):
        pack_q(ahead(r, step))
    own_q = pltpu.make_async_copy(qs.at[r], qg.at[r], own_sem.at[1])
    own_q.start()
    for step in range(1, ROW):
        kv_copy(step).wait_recv()
        pass_up(step)
        if step == Q_AFTER:
            for other in range(1, ROW):
                q_copy(other).start()
    for step in range(1, ROW):
        q_copy(step).wait_recv()

    @pl.when(row == 1)
    def _():
        for step in range(ROW):
            up_copy(step).wait_recv()

    @pl.when(row == 0)
    def _():
        for step in range(ROW):
            up_copy(step).wait_send()

    for step in range(1, ROW):
        kv_copy(step).wait_send()
        q_copy(step).wait_send()
    own_kv.wait()
    own_q.wait()


def spread(kept, q, k, v):
    rows = q.shape[0]
    anywhere = pl.BlockSpec(memory_space=pl.ANY)
    bf16 = jnp.bfloat16
    dma = pltpu.SemaphoreType.DMA
    return pl.pallas_call(
        spread_kernel,
        out_shape=(
            jax.ShapeDtypeStruct((ROW, HEAD_DIM, SLOTS * 2 * BLK), bf16),
            jax.ShapeDtypeStruct((2 * ROW, 2 * SLOTS * BLK, HEAD_DIM), bf16),
        ),
        in_specs=[pl.BlockSpec(memory_space=pltpu.SMEM), anywhere, anywhere, anywhere],
        out_specs=(anywhere, anywhere),
        scratch_shapes=[
            pltpu.VMEM((rows, HEADS * HEAD_DIM), bf16),
            pltpu.VMEM((rows, KV_HEADS * HEAD_DIM), bf16),
            pltpu.VMEM((rows, KV_HEADS * HEAD_DIM), bf16),
            pltpu.VMEM((ROW, HEAD_DIM, SLOTS * 2 * BLK), bf16),
            pltpu.VMEM((ROW, 2 * SLOTS * BLK, HEAD_DIM), bf16),
            dma((3,)), dma((ROW,)), dma((ROW,)), dma((ROW,)), dma((ROW,)), dma((ROW,)), dma((ROW,)), dma((2,)),
        ],
        compiler_params=pltpu.CompilerParams(
            collective_id=1, has_side_effects=True, vmem_limit_bytes=60 << 20
        ),
        name="spread",
    )(kept, q, k, v)


def attend_kernel(
    parents_ref, kept_ref, qg, kvg, og,
    q_v, kv_v, o_v, bias_ref, up_ref, base_ref, list_ref, seen_ref, size_ref, in_sem, out_sem,
):
    c, row, r = place()
    half = ROW * 2 * SLOTS * BLK
    load_own = pltpu.make_async_copy(kvg.at[half:], kv_v.at[half:], in_sem.at[0])
    load_low = pltpu.make_async_copy(kvg.at[:half], kv_v.at[:half], in_sem.at[1])
    load_q = pltpu.make_async_copy(qg, q_v, in_sem.at[2])
    load_q.start()
    load_own.start()

    @pl.when(row == 1)
    def _():
        load_low.start()

    end = BLOCKS
    reach = WINDOW // BLK
    first_tile = row * ROW * TILES_DEV

    up_ref[end] = -BLOCKS * 4
    up_ref[0] = end
    for t in range(1, BLOCKS):
        p = parents_ref[t]
        up_ref[t] = jnp.where(kept_ref[p] > 0, p, up_ref[p])
    base_ref[end] = half
    for s in range(BLOCKS // TILES_DEV):
        lin = jnp.clip(s - ROW * row + ROW, 0, 2 * ROW - 1) * (2 * SLOTS * BLK)
        before = jnp.int32(0)
        for j in range(TILES_DEV):
            t = s * TILES_DEV + j
            base_ref[t] = lin + jnp.minimum(before, SLOTS - 1) * BLK
            before = before + jnp.where(kept_ref[t] > 0, 1, 0)
    count = jnp.int32(0)
    for j in range(ROW * TILES_DEV):
        t = first_tile + j
        list_ref[count] = t
        count = count + jnp.where(kept_ref[t] > 0, 1, 0)

    def gather(i, _):
        t = list_ref[i]

        def visit(state):
            node, k = state
            seen_ref[i * MOST + k] = base_ref[node] + jnp.where(t - node == reach, 2, 0)
            nxt = up_ref[node]
            return jnp.where(nxt >= t - reach, nxt, end), k + 1

        _, k = lax.while_loop(lambda state: state[0] < end, visit, (t, jnp.int32(0)))
        size_ref[i] = k
        for extra in range(PAD):
            seen_ref[i * MOST + k + extra] = base_ref[end] + 1
        return 0

    lax.fori_loop(0, count, gather, 0)
    rc = lax.broadcasted_iota(jnp.int32, (BLK, BLK), 1) - lax.broadcasted_iota(jnp.int32, (BLK, BLK), 0)
    bias_ref[0] = jnp.zeros((BLK, BLK), jnp.float32)
    bias_ref[1] = jnp.full((BLK, BLK), NEG, jnp.float32)
    bias_ref[2] = jnp.where(rc < 0, 0.0, NEG)
    bias_ref[3] = jnp.where(rc >= 0, 0.0, NEG)
    load_q.wait()
    load_own.wait()

    @pl.when(row == 1)
    def _():
        load_low.wait()

    def some(width, first, j, _):
        which = [jnp.minimum(first + width * j + n, count - 1) for n in range(width)]
        spots, heads = [], []
        for i in which:
            t = list_ref[i]
            slot = (base_ref[t] // BLK) % SLOTS
            shard = (t - first_tile) // TILES_DEV
            spots.append((shard, pl.multiple_of(slot * BLK, BLK)))
            heads.append(q_v[shard, :, pl.ds(pl.multiple_of(slot * 2 * BLK, 2 * BLK), 2 * BLK)])
        longest = functools.reduce(jnp.maximum, [size_ref[i] for i in which])

        def over(size):
            parts = [[] for _ in which]
            tops = [None for _ in which]
            values = [[] for _ in which]
            for n, i in enumerate(which):
                for g in range(size):
                    entry = seen_ref[i * MOST + g]
                    base = pl.multiple_of(entry // BLK * BLK, BLK)
                    bias = bias_ref[3 if g == 0 else entry % BLK]
                    s = jnp.dot(kv_v[pl.ds(base, BLK), :], heads[n], preferred_element_type=jnp.float32) * SCALE
                    s = s + jnp.concatenate([bias, bias], 1)
                    fold = jnp.max(s.reshape(BLK // 8, 8, 2 * BLK), axis=0)
                    tops[n] = fold if g == 0 else jnp.maximum(tops[n], fold)
                    parts[n].append(s)
                    values[n].append(kv_v[pl.ds(base + SLOTS * BLK, BLK), :])
            tops = [jnp.max(top, axis=0, keepdims=True) for top in tops]
            accs, totals = [], []
            for n in range(width):
                weights, total = [], None
                for part in parts[n]:
                    term = jnp.exp2(part - tops[n])
                    fold = jnp.sum(term.reshape(BLK // 8, 8, 2 * BLK), axis=0)
                    total = fold if total is None else total + fold
                    weights.append(term.astype(jnp.bfloat16))
                totals.append(jnp.sum(total, axis=0, keepdims=True))
                w = jnp.concatenate(weights, 0)
                accs.append(jnp.dot(jnp.concatenate(values[n], 1), w, preferred_element_type=jnp.float32))
            outs = [(acc / total).astype(jnp.bfloat16) for acc, total in zip(accs, totals)]
            outs = [jnp.concatenate([o[:, :BLK].T, o[:, BLK:].T], 1) for o in outs]
            for i, o in zip(which, outs):
                o_v[i] = o

        for low, size in zip((0, *SIZES), SIZES):
            pl.when((longest > low) & (longest <= size))(functools.partial(over, size))
        for n in range(width):

            @pl.when(first + width * j + n < count)
            def _():
                shard, at = spots[n]
                pltpu.make_async_copy(
                    o_v.at[which[n]], og.at[shard, pl.ds(at, BLK), :], out_sem.at[which[n]]
                ).start()

        return 0

    many = (count + 1) // WIDE
    lax.fori_loop(0, many, functools.partial(some, WIDE, 0), 0)
    left = jnp.maximum(count - WIDE * many, 0)
    lax.fori_loop(0, (left + NARROW - 1) // NARROW, functools.partial(some, NARROW, WIDE * many), 0)

    def drain(w, _):
        pltpu.make_async_copy(o_v.at[w], og.at[0, pl.ds(0, BLK), :], out_sem.at[w]).wait()
        return 0

    lax.fori_loop(0, count, drain, 0)


def attend(parents, kept, qg, kvg):
    smem = pl.BlockSpec(memory_space=pltpu.SMEM)
    anywhere = pl.BlockSpec(memory_space=pl.ANY)
    bf16 = jnp.bfloat16
    rows = 2 * ROW * 2 * SLOTS * BLK
    return pl.pallas_call(
        attend_kernel,
        out_shape=jax.ShapeDtypeStruct((ROW, SLOTS * BLK, GROUP), bf16),
        in_specs=[smem, smem, anywhere, anywhere],
        out_specs=anywhere,
        scratch_shapes=[
            pltpu.VMEM((ROW, HEAD_DIM, SLOTS * 2 * BLK), bf16),
            pltpu.VMEM((rows, HEAD_DIM), bf16),
            pltpu.VMEM((ROW * SLOTS, BLK, GROUP), bf16),
            pltpu.VMEM((4, BLK, BLK), jnp.float32),
            pltpu.SMEM((BLOCKS + 1,), jnp.int32),
            pltpu.SMEM((BLOCKS + 1,), jnp.int32),
            pltpu.SMEM((ROW * TILES_DEV + 1,), jnp.int32),
            pltpu.SMEM((ROW * SLOTS * MOST + PAD,), jnp.int32),
            pltpu.SMEM((ROW * SLOTS,), jnp.int32),
            pltpu.SemaphoreType.DMA((3,)),
            pltpu.SemaphoreType.DMA((ROW * SLOTS,)),
        ],
        compiler_params=pltpu.CompilerParams(vmem_limit_bytes=60 << 20),
        name="attend",
    )(parents, kept, qg, kvg.reshape(rows, HEAD_DIM))


def collect_kernel(og, oc, send, recv, own_sem):
    _, row, r = place()
    barrier = pltpu.get_barrier_semaphore()
    for step in range(1, ROW):
        pl.semaphore_signal(barrier, 1, device_id=peer(row, (r + step) % ROW), device_id_type=MESH)
    own = pltpu.make_async_copy(og.at[r], oc.at[r], own_sem)
    own.start()
    pl.semaphore_wait(barrier, ROW - 1)
    copies = []
    for step in range(1, ROW):
        to = (r + step) % ROW
        copies.append(
            pltpu.make_async_remote_copy(
                og.at[to], oc.at[r], send.at[step], recv.at[step],
                device_id=peer(row, to), device_id_type=MESH,
            )
        )
    for copy in copies:
        copy.start()
    for copy in copies:
        copy.wait_recv()
    for copy in copies:
        copy.wait_send()
    own.wait()


def collect(og):
    anywhere = pl.BlockSpec(memory_space=pl.ANY)
    return pl.pallas_call(
        collect_kernel,
        out_shape=jax.ShapeDtypeStruct((ROW, SLOTS * BLK, GROUP), jnp.bfloat16),
        in_specs=[anywhere],
        out_specs=anywhere,
        scratch_shapes=[
            pltpu.SemaphoreType.DMA((ROW,)), pltpu.SemaphoreType.DMA((ROW,)), pltpu.SemaphoreType.DMA,
        ],
        compiler_params=pltpu.CompilerParams(
            collective_id=2, has_side_effects=True, vmem_limit_bytes=60 << 20
        ),
        name="collect",
    )(og)


def expand_kernel(kept_ref, oc, out, wide, sem):
    c, _, _ = place()
    copies = []
    before = jnp.bool_(False)
    for j in range(TILES_DEV):
        rows = slice(j * BLK, (j + 1) * BLK)
        kept = kept_ref[c * TILES_DEV + j] > 0
        slot = pl.multiple_of(jnp.where(before, BLK, 0), BLK)

        @pl.when(kept)
        def _():
            for h in range(ROW):
                wide[rows, h * GROUP : (h + 1) * GROUP] = oc[h, pl.ds(slot, BLK), :]

        @pl.when(jnp.logical_not(kept))
        def _():
            wide[rows, :] = jnp.zeros((BLK, HEADS * HEAD_DIM), jnp.bfloat16)

        before = before | kept
        copies.append(pltpu.make_async_copy(wide.at[rows], out.at[rows], sem.at[j]))
        copies[-1].start()
    for copy in copies:
        copy.wait()


def expand(kept, oc):
    rows = TILES_DEV * BLK
    return pl.pallas_call(
        expand_kernel,
        out_shape=jax.ShapeDtypeStruct((rows, HEADS * HEAD_DIM), jnp.bfloat16),
        in_specs=[pl.BlockSpec(memory_space=pltpu.SMEM), pl.BlockSpec(memory_space=pltpu.VMEM)],
        out_specs=pl.BlockSpec(memory_space=pl.ANY),
        scratch_shapes=[
            pltpu.VMEM((rows, HEADS * HEAD_DIM), jnp.bfloat16), pltpu.SemaphoreType.DMA((TILES_DEV,)),
        ],
        name="expand",
    )(kept, oc)


def body(queries, key_rows, value_rows, parents, kept_tiles):
    qg, kvg = spread(kept_tiles, queries, key_rows, value_rows)
    og = attend(parents, kept_tiles, qg, kvg)
    return expand(kept_tiles, collect(og))


def solution(mesh):
    return jax.shard_map(
        body,
        mesh=mesh,
        in_specs=(
            P(("dp", "ctx"), None),
            P(("dp", "ctx"), None),
            P(("dp", "ctx"), None),
            P("dp"),
            P("dp"),
        ),
        out_specs=P(("dp", "ctx"), None),
        check_vma=False,
    )
```
